32 devices in a mesh: gx: 8 (over z, x), yz: 4 (over y, core).
Axes of the slice: x: 2, y: 2, z: 4, core: 2. Of those that a mesh axis runs over, the one named last changes fastest.
Arguments:
- residuals: float32 [32, 3, 64, 32, 128], P(None, None, 'gx', 'yz'), may hold values from -6 to 6
- vectors: float32 [8, 3, 64, 32, 128], P(None, None, 'gx', 'yz'), may hold values from -0.05 to 1.6
- phases: int32 [64, 32, 128], P('gx', 'yz'), may hold values from 0 to 7
- stiffness: float32 [8], replicated, may hold values from 0.5 to 4
Outputs:
- coarse_coeffs: float32 [256, 32], P(('gx', 'yz'))
- preconditioned: float32 [32, 3, 64, 32, 128], P(None, None, 'gx', 'yz')
The draws below stay inside these ranges and needn't reach their ends.
All inputs are finite; a program needn't handle non-finite values.
Results may differ from the reference program's by a relative error of at most 0.0003.
Values sent between devices are 32-bit elements; how exact they have to be, the bound alone decides.
A program may use at most 192 MiB of HBM per device.

```python
import math
import jax
import jax.numpy as jnp
from jax import lax

K = 8
PHASES = 8
CX = 8
CY = 8
CZ = 128
RHS = 32
SWEEPS = 4
NX = 64
NY = 32
N_GX = 8
N_YZ = 4


def draw_vectors(key, part):
    first_key, second_key = jax.random.split(jax.random.fold_in(key, 17))
    means = jax.random.uniform(first_key, (K, 3, 1, 1, 1), jnp.float32, 0.2, 1.0)
    rough = jnp.clip(0.05 * jax.random.normal(second_key, (K, 3, NX, NY, CZ), jnp.float32), -0.25, 0.25)
    return means + rough


def set_ends(result, rng, smallest, top_value):
    spot = [jax.random.randint(jax.random.fold_in(rng, axis), (), 0, length) for axis, length in enumerate(result.shape)]
    main_axis = result.shape.index(max(result.shape))
    next_to = spot[:main_axis] + [(spot[main_axis] + 1) % result.shape[main_axis]] + spot[main_axis + 1:]
    return result.at[tuple(spot)].set(smallest).at[tuple(next_to)].set(top_value)


def level_of(own_key, shape, cuts, smallest, top_value):
    factor_of, own = 1.0, jax.random.fold_in(own_key, 6)
    for dim, blocks in cuts:
        steps = jnp.exp(jax.random.uniform(jax.random.fold_in(own, dim), (blocks,), jnp.float32, smallest / len(cuts), top_value / len(cuts)))
        factor_of = factor_of * jnp.repeat(steps, shape[dim] // blocks).reshape([-1 if axis == dim else 1 for axis in range(len(shape))])
    return factor_of


def scatter_about(rng, dims, deviation, limit, shards=(), held_as=jnp.bfloat16):
    drawn = jax.random.normal(rng, dims, jnp.float32) * deviation
    if len(shards) > 0:
        drawn = level_of(rng, dims, shards, -0.22, 0.18) * drawn
    return jnp.clip(drawn, min=-limit, max=limit).astype(held_as)


def setup_inputs(seed: int = 0) -> dict:
    arg_keys = jax.random.split(jax.random.key(seed), 5)
    return {
        "residuals": scatter_about(arg_keys[0], (RHS, 3, NX, NY, CZ), 1.0, 6.0, ((2, 8), (3, 4)), jnp.float32),
        "vectors": draw_vectors(jax.random.fold_in(arg_keys[4], 71), 0),
        "phases": set_ends(jax.random.randint(arg_keys[2], (NX, NY, CZ), 0, PHASES), jax.random.fold_in(arg_keys[2], 1), 0, PHASES - 1).astype(jnp.int32),
        "stiffness": jnp.clip(jnp.exp(jax.random.uniform(arg_keys[3], (PHASES,), jnp.float32, math.log(0.5), math.log(4.0))), 0.5, 4.0),
    }


HIGH = lax.Precision.HIGHEST

def face_weights(modulus_ext):
    centre = modulus_ext[1:-1, 1:-1, :]
    zpadded = jnp.pad(centre, ((0, 0), (0, 0), (1, 1)))
    west_side = 0.5 * (centre + modulus_ext[:-2, 1:-1, :])
    east_side = 0.5 * (centre + modulus_ext[2:, 1:-1, :])
    south_side = 0.5 * (centre + modulus_ext[1:-1, :-2, :])
    north_side = 0.5 * (centre + modulus_ext[1:-1, 2:, :])
    lower_side = 0.5 * (centre + zpadded[:, :, :-2])
    upper_side = 0.5 * (centre + zpadded[:, :, 2:])
    diagonal_sum = 0.002 + west_side + east_side + south_side + north_side + lower_side + upper_side
    return (diagonal_sum, west_side, east_side, south_side, north_side, lower_side, upper_side)

def operate(values, weights):
    diagonal_sum, west_side, east_side, south_side, north_side, lower_side, upper_side = weights
    centre = values[..., 1:-1, 1:-1, :]
    spacing = [(0, 0)] * (values.ndim - 1) + [(1, 1)]
    zpadded = jnp.pad(centre, spacing)
    beside = west_side * values[..., :-2, 1:-1, :] + east_side * values[..., 2:, 1:-1, :]
    beside = beside + south_side * values[..., 1:-1, :-2, :] + north_side * values[..., 1:-1, 2:, :]
    beside = beside + lower_side * zpadded[..., :-2] + upper_side * zpadded[..., 2:]
    return diagonal_sum * centre - beside

def coarse_blocks(vectors_ext, modulus_ext):
    weights = face_weights(modulus_ext[1:-1, 1:-1, :])
    own_cells = vectors_ext[:, :, 2:-2, 2:-2, :]
    isolated = jnp.pad(own_cells, ((0, 0), (0, 0), (1, 1), (1, 1), (0, 0)))
    applied = operate(isolated, weights)
    self_block = jnp.einsum('kcxyz,lcxyz->kl', own_cells, applied, precision=HIGH)
    west_block = -jnp.einsum('kcyz,lcyz->kl', weights[1][0] * own_cells[:, :, 0], vectors_ext[:, :, 1, 2:-2, :], precision=HIGH)
    east_block = -jnp.einsum('kcyz,lcyz->kl', weights[2][-1] * own_cells[:, :, -1], vectors_ext[:, :, -2, 2:-2, :], precision=HIGH)
    south_block = -jnp.einsum('kcxz,lcxz->kl', weights[3][:, 0] * own_cells[:, :, :, 0], vectors_ext[:, :, 2:-2, 1, :], precision=HIGH)
    north_block = -jnp.einsum('kcxz,lcxz->kl', weights[4][:, -1] * own_cells[:, :, :, -1], vectors_ext[:, :, 2:-2, -2, :], precision=HIGH)
    return jnp.stack([self_block, west_block, east_block, south_block, north_block])

def assemble(blocks, stride):
    count = blocks.shape[0]
    width = blocks.shape[2]
    rows_index = jnp.arange(count, dtype=jnp.int32)
    assembled = jnp.zeros((count, width, count, width), jnp.float32)
    for slot_index, offset in enumerate((0, -stride, stride, -1, 1)):
        select = (rows_index[None, :] == rows_index[:, None] + offset).astype(jnp.float32)
        assembled = assembled + blocks[:, slot_index][:, :, None, :] * select[:, None, :, None]
    return assembled.reshape(count * width, count * width)

def local_solve(deflated_ext, modulus_ext):
    weights = face_weights(modulus_ext)
    inner_mod = modulus_ext[1:-1, 1:-1, :]
    width_x = inner_mod.shape[0]
    width_y = inner_mod.shape[1]
    x_index = jnp.arange(width_x)[:, None]
    y_index = jnp.arange(width_y)[None, :]
    x_edge = (x_index == 0) | (x_index == width_x - 1)
    y_edge = (y_index == 0) | (y_index == width_y - 1)
    corner = x_edge & y_edge
    active = ((inner_mod > 0) & jnp.logical_not(corner[:, :, None])).astype(jnp.float32)
    approx = jnp.zeros_like(deflated_ext)
    for repeat in range(SWEEPS):
        padded = jnp.pad(approx, ((0, 0), (0, 0), (1, 1), (1, 1), (0, 0)))
        approx = active * (approx + 0.8 * (deflated_ext - operate(padded, weights)) / weights[0])
    return approx[:, :, 1:-1, 1:-1, :]

def reference(residuals, vectors, phases, stiffness):
    count = N_GX * N_YZ
    modulus = jnp.take(stiffness, phases, axis=0)
    modulus_pad = jnp.pad(modulus, ((2, 2), (2, 2), (0, 0)))
    vectors_pad = jnp.pad(vectors, ((0, 0), (0, 0), (2, 2), (2, 2), (0, 0)))
    zero_index = jnp.zeros((), jnp.int32)
    block_ids = jnp.arange(count, dtype=jnp.int32)

    def starts(block_index):
        x_start = (block_index // N_YZ * CX).astype(jnp.int32)
        y_start = (block_index % N_YZ * CY).astype(jnp.int32)
        return (x_start, y_start)

    def coarse_part(block_index):
        x_start, y_start = starts(block_index)
        modulus_ext = lax.dynamic_slice(modulus_pad, (x_start, y_start, zero_index), (CX + 4, CY + 4, CZ))
        vectors_ext = lax.dynamic_slice(vectors_pad, (zero_index, zero_index, x_start, y_start, zero_index), (K, 3, CX + 4, CY + 4, CZ))
        own_res = lax.dynamic_slice(residuals, (zero_index, zero_index, x_start, y_start, zero_index), (RHS, 3, CX, CY, CZ))
        own_vec = vectors_ext[:, :, 2:-2, 2:-2, :]
        rhs_part = jnp.einsum('kcxyz,rcxyz->kr', own_vec, own_res, precision=HIGH)
        return (coarse_blocks(vectors_ext, modulus_ext), rhs_part)
    blocks, rhs_parts = lax.map(coarse_part, block_ids)
    matrix = assemble(blocks, N_YZ)
    coarse_rhs = rhs_parts.reshape(count * K, RHS)
    factor = jnp.linalg.cholesky(matrix)
    coarse_coeffs = jax.scipy.linalg.cho_solve((factor, True), coarse_rhs)
    coeff_grid = coarse_coeffs.reshape(N_GX, N_YZ, K, RHS)
    vector_grid = vectors.reshape(K, 3, N_GX, CX, N_YZ, CY, CZ)
    correction = jnp.einsum('gqkr,kcgaqbz->rcgaqbz', coeff_grid, vector_grid, precision=HIGH).reshape(RHS, 3, NX, NY, CZ)
    corr_pad = jnp.pad(correction, ((0, 0), (0, 0), (2, 2), (2, 2), (0, 0)))
    res_pad = jnp.pad(residuals, ((0, 0), (0, 0), (1, 1), (1, 1), (0, 0)))

    def local_block(block_index):
        x_start, y_start = starts(block_index)
        modulus_ext = lax.dynamic_slice(modulus_pad, (x_start, y_start, zero_index), (CX + 4, CY + 4, CZ))
        corr_ext = lax.dynamic_slice(corr_pad, (zero_index, zero_index, x_start, y_start, zero_index), (RHS, 3, CX + 4, CY + 4, CZ))
        res_ext = lax.dynamic_slice(res_pad, (zero_index, zero_index, x_start, y_start, zero_index), (RHS, 3, CX + 2, CY + 2, CZ))
        deflated_ext = res_ext - operate(corr_ext, face_weights(modulus_ext))
        local_part = local_solve(deflated_ext, modulus_ext)
        return corr_ext[:, :, 2:-2, 2:-2, :] + local_part
    pieces = lax.map(local_block, block_ids)
    preconditioned = pieces.reshape(N_GX, N_YZ, RHS, 3, CX, CY, CZ).transpose(2, 3, 0, 4, 1, 5, 6).reshape(RHS, 3, NX, NY, CZ)
    return (coarse_coeffs, preconditioned)
```

```python
import functools

import jax
import jax.numpy as jnp
from jax import lax
from jax.experimental import pallas as pl
from jax.experimental.pallas import tpu as pltpu
from jax.sharding import PartitionSpec as P

SWEEPS = 4


HIGH = lax.Precision.HIGHEST


def extended(cells, sides, width):
    for axis, dim in sides:
        count = lax.axis_size(axis)
        ends = count - 1
        head = lax.slice_in_dim(cells, 0, width, axis=dim)
        tail = lax.slice_in_dim(cells, cells.shape[dim] - width, cells.shape[dim], axis=dim)
        cells = jnp.concatenate(
            [
                lax.ppermute(tail, axis, [(i, (i + 1) % count) for i in range(ends)]),
                cells,
                lax.ppermute(head, axis, [((i + 1) % count, i) for i in range(ends)]),
            ],
            axis=dim,
        )
    return cells


def face_weights(modulus_ext):
    centre = modulus_ext[1:-1, 1:-1, :]
    zpadded = jnp.pad(centre, ((0, 0), (0, 0), (1, 1)))
    west_side = 0.5 * (centre + modulus_ext[:-2, 1:-1, :])
    east_side = 0.5 * (centre + modulus_ext[2:, 1:-1, :])
    south_side = 0.5 * (centre + modulus_ext[1:-1, :-2, :])
    north_side = 0.5 * (centre + modulus_ext[1:-1, 2:, :])
    lower_side = 0.5 * (centre + zpadded[:, :, :-2])
    upper_side = 0.5 * (centre + zpadded[:, :, 2:])
    diagonal_sum = 0.002 + west_side + east_side + south_side + north_side + lower_side + upper_side
    return (diagonal_sum, west_side, east_side, south_side, north_side, lower_side, upper_side)


def operate(values, weights):
    diagonal_sum, west_side, east_side, south_side, north_side, lower_side, upper_side = weights
    centre = values[..., 1:-1, 1:-1, :]
    spacing = [(0, 0)] * (values.ndim - 1) + [(1, 1)]
    zpadded = jnp.pad(centre, spacing)
    beside = west_side * values[..., :-2, 1:-1, :] + east_side * values[..., 2:, 1:-1, :]
    beside = beside + south_side * values[..., 1:-1, :-2, :] + north_side * values[..., 1:-1, 2:, :]
    beside = beside + lower_side * zpadded[..., :-2] + upper_side * zpadded[..., 2:]
    return diagonal_sum * centre - beside


def coarse_blocks(vectors_ext, modulus_ext):
    weights = face_weights(modulus_ext[1:-1, 1:-1, :])
    own_cells = vectors_ext[:, :, 2:-2, 2:-2, :]
    isolated = jnp.pad(own_cells, ((0, 0), (0, 0), (1, 1), (1, 1), (0, 0)))
    applied = operate(isolated, weights)
    self_block = jnp.einsum("kcxyz,lcxyz->kl", own_cells, applied, precision=HIGH)
    west_block = -jnp.einsum(
        "kcyz,lcyz->kl",
        weights[1][0] * own_cells[:, :, 0],
        vectors_ext[:, :, 1, 2:-2, :],
        precision=HIGH,
    )
    east_block = -jnp.einsum(
        "kcyz,lcyz->kl",
        weights[2][-1] * own_cells[:, :, -1],
        vectors_ext[:, :, -2, 2:-2, :],
        precision=HIGH,
    )
    south_block = -jnp.einsum(
        "kcxz,lcxz->kl",
        weights[3][:, 0] * own_cells[:, :, :, 0],
        vectors_ext[:, :, 2:-2, 1, :],
        precision=HIGH,
    )
    north_block = -jnp.einsum(
        "kcxz,lcxz->kl",
        weights[4][:, -1] * own_cells[:, :, :, -1],
        vectors_ext[:, :, 2:-2, -2, :],
        precision=HIGH,
    )
    return jnp.stack([self_block, west_block, east_block, south_block, north_block])


MESH = pl.DeviceIdType.MESH


def eliminate(rows, size):
    sublane = lax.broadcasted_iota(jnp.int32, rows[0].shape, 0)
    for p in range(size):
        reduced = []
        for a in rows:
            column = jnp.broadcast_to(a[:, p : p + 1], a.shape)
            pivot = a[p : p + 1, :] / column[p : p + 1, :]
            reduced.append(jnp.where(sublane == p, pivot, a - column * pivot))
        rows = reduced
    return rows


def product(a, b):
    return jnp.dot(a, b, precision=HIGH, preferred_element_type=jnp.float32)


def cyclic_solve(rows, size):
    count = len(rows)
    width = rows[0].shape[1]
    lane = lax.broadcasted_iota(jnp.int32, rows[0].shape, 1)
    is_own = lane < size
    is_low = (lane >= size) & (lane < 2 * size)
    is_high = (lane >= 2 * size) & (lane < 3 * size)
    is_rhs = lane >= 3 * size
    live = list(range(count))
    system = dict(enumerate(rows))
    levels = []
    while len(live) > 1:
        out = live[1::2]
        kept = live[0::2]
        solved = dict(zip(out, eliminate([system[i] for i in out], size)))
        fresh = {}
        for place, i in enumerate(kept):
            a = system[i]
            total = jnp.where(is_own | is_rhs, a, 0.0)
            if place > 0:
                t = product(a[:, size : 2 * size], solved[out[place - 1]])
                shifted = pltpu.roll(t, width - 2 * size, 1)
                total = total - jnp.where(is_own, shifted, jnp.where(is_low | is_rhs, t, 0.0))
            if place < len(out):
                t = product(a[:, 2 * size : 3 * size], solved[out[place]])
                shifted = pltpu.roll(t, width - size, 1)
                total = total - jnp.where(is_own, shifted, jnp.where(is_high | is_rhs, t, 0.0))
            fresh[i] = total
        levels.append((live, out, solved))
        system = fresh
        live = kept
    last = eliminate([system[live[0]]], size)[0]
    answer = {live[0]: last[:, 3 * size :]}
    for before, out, solved in reversed(levels):
        for i in out:
            a = solved[i]
            place = before.index(i)
            x = a[:, 3 * size :] - product(a[:, size : 2 * size], answer[before[place - 1]])
            if place + 1 < len(before):
                x = x - product(a[:, 2 * size : 3 * size], answer[before[place + 1]])
            answer[i] = x
    return [answer[i] for i in range(count)]


def coarse_kernel(
    count_x, count_y, width, panel, res, south_face, north_face,
    coeffs, grid, halo_x, halo_y, gathered, send_sem, recv_sem, halo_send, halo_recv
):
    index_x = lax.axis_index("gx")
    index_y = lax.axis_index("yz")
    count = count_x * count_y
    me = index_x * count_y + index_y
    barrier = pltpu.get_barrier_semaphore()

    def greet(step, carry):
        other = lax.rem(me + step, count)
        pl.semaphore_signal(
            barrier, inc=1, device_id=(other // count_y, lax.rem(other, count_y)), device_id_type=MESH
        )
        return carry

    lax.fori_loop(1, count, greet, 0)
    pl.semaphore_wait(barrier, count - 1)

    def sending(other, slot):
        return pltpu.make_async_remote_copy(
            src_ref=panel,
            dst_ref=gathered.at[slot],
            send_sem=send_sem.at[other],
            recv_sem=recv_sem.at[slot],
            device_id=(other // count_y, lax.rem(other, count_y)),
            device_id_type=MESH,
        )

    def send(step, carry):
        sending(lax.rem(me + step, count), me).start()
        return carry

    lax.fori_loop(1, count, send, 0)
    depth = res.shape[2]
    faces = (
        (index_x > 0, index_x < count_x - 1, res.at[:, :, 0], halo_x.at[1], (index_x - 1, index_y)),
        (index_x < count_x - 1, index_x > 0, res.at[:, :, depth - 1], halo_x.at[0], (index_x + 1, index_y)),
        (index_y > 0, index_y < count_y - 1, south_face, halo_y.at[1], (index_x, index_y - 1)),
        (index_y < count_y - 1, index_y > 0, north_face, halo_y.at[0], (index_x, index_y + 1)),
    )
    copies = []
    for slot, (sends, receives, source, target, device) in enumerate(faces):
        copy = pltpu.make_async_remote_copy(
            src_ref=source,
            dst_ref=target,
            send_sem=halo_send.at[slot],
            recv_sem=halo_recv.at[slot],
            device_id=device,
            device_id_type=MESH,
        )
        pl.when(sends)(copy.start)
        copies.append((sends, receives, copy))
    gathered[me] = panel[...]

    def collect(step, carry):
        other = lax.rem(me + step, count)
        sending(other, other).wait_recv()
        return carry

    lax.fori_loop(1, count, collect, 0)
    size = count_y * width
    rows = [
        gathered[pl.ds(g * count_y, count_y)].reshape(size, panel.shape[1]) for g in range(count_x)
    ]
    for g, x in enumerate(cyclic_solve(rows, size)):
        coeffs[pl.ds(g * size, size), :] = x
    slot = 0
    for step_x in (-1, 0, 1):
        for step_y in (-1, 0, 1):
            near_x = jnp.clip(index_x + step_x, 0, count_x - 1)
            near_y = jnp.clip(index_y + step_y, 0, count_y - 1)
            start = pl.multiple_of((near_x * count_y + near_y) * width, width)
            grid[pl.ds(slot * width, width), :] = coeffs[pl.ds(start, width), :]
            slot += 1

    def drain(step, carry):
        sending(lax.rem(me + step, count), me).wait_send()
        return carry

    lax.fori_loop(1, count, drain, 0)
    for sends, receives, copy in copies:
        pl.when(sends)(copy.wait_send)
        pl.when(receives)(copy.wait_recv)


def coarse_solve(panel, residuals, count_x, count_y, width):
    rhs, parts, depth, breadth, length = residuals.shape
    count = count_x * count_y
    vmem = pl.BlockSpec(memory_space=pltpu.VMEM)
    hbm = pl.BlockSpec(memory_space=pl.ANY)
    return pl.pallas_call(
        functools.partial(coarse_kernel, count_x, count_y, width),
        out_shape=(
            jax.ShapeDtypeStruct((count * width, rhs), jnp.float32),
            jax.ShapeDtypeStruct((9 * width, rhs), jnp.float32),
            jax.ShapeDtypeStruct((2, rhs, parts, breadth, length), jnp.float32),
            jax.ShapeDtypeStruct((2, rhs, parts, depth, length), jnp.float32),
        ),
        in_specs=[vmem, hbm, hbm, hbm],
        out_specs=(vmem, vmem, hbm, hbm),
        scratch_shapes=[
            pltpu.VMEM((count,) + panel.shape, jnp.float32),
            pltpu.SemaphoreType.DMA((count,)),
            pltpu.SemaphoreType.DMA((count,)),
            pltpu.SemaphoreType.DMA((4,)),
            pltpu.SemaphoreType.DMA((4,)),
        ],
        compiler_params=pltpu.CompilerParams(collective_id=0, has_side_effects=True),
    )(panel, residuals, residuals[:, :, :, 0, :], residuals[:, :, :, -1, :])


def panel_row(blocks, coarse_rhs, count_y):
    width = blocks.shape[1]
    columns = jnp.arange(count_y, dtype=jnp.int32)
    index_y = lax.axis_index("yz")

    def placed(block, offset):
        select = (columns == index_y + offset).astype(jnp.float32)
        return (block[:, None, :] * select[None, :, None]).reshape(width, count_y * width)

    own = placed(blocks[0], 0) + placed(blocks[3], -1) + placed(blocks[4], 1)
    return jnp.concatenate([own, placed(blocks[1], 0), placed(blocks[2], 0), coarse_rhs], axis=1)


def schwarz_kernel(
    rhs, parts, depth, breadth, width, res, vec, weights, cgrid, halo_x, halo_y, out,
    coeff, corr, forced, first, second
):
    length = res.shape[1]
    wide = breadth + 4
    own = depth * breadth

    for cls in range(9):
        for k in range(width):
            coeff[cls * width + k] = jnp.broadcast_to(
                cgrid[:, cls * width + k : cls * width + k + 1], (rhs, length)
            )
    zero = jnp.zeros((rhs, length), jnp.float32)
    for buffer in (first, second):
        def clear(i, carry, buffer=buffer):
            buffer[i] = zero
            return carry

        lax.fori_loop(0, (depth + 4) * wide, clear, 0)

    def component(part, carry):
        def region(cls, x0, nx, y0, ny):
            def one(i, carry):
                cell = (x0 + i // ny) * wide + y0 + lax.rem(i, ny)
                value = coeff[cls * width] * vec[part, cell, pl.ds(0, 1), :]
                for k in range(1, width):
                    value = value + coeff[cls * width + k] * vec[part, cell, pl.ds(k, 1), :]
                corr[cell] = value
                return carry

            lax.fori_loop(0, nx * ny, one, 0, unroll=2 if nx * ny > 1 else 1)

        spans_x = ((0, 2), (2, depth), (depth + 2, 2))
        spans_y = ((0, 2), (2, breadth), (breadth + 2, 2))
        for a, (x0, nx) in enumerate(spans_x):
            for b, (y0, ny) in enumerate(spans_y):
                if a != 1 and b != 1:
                    region(a * 3 + b, 1 if a == 0 else x0, 1, 1 if b == 0 else y0, 1)
                else:
                    region(a * 3 + b, x0, nx, y0, ny)

        def beside(buffer, x, y):
            cell = x * wide + y
            w = (x - 1) * (breadth + 2) + y - 1
            centre = buffer[cell]
            total = weights[w, pl.ds(1, 1), :] * buffer[cell - wide]
            total = total + weights[w, pl.ds(2, 1), :] * buffer[cell + wide]
            total = total + weights[w, pl.ds(3, 1), :] * buffer[cell - 1]
            total = total + weights[w, pl.ds(4, 1), :] * buffer[cell + 1]
            total = total + weights[w, pl.ds(5, 1), :] * pltpu.roll(centre, 1, 1)
            total = total + weights[w, pl.ds(6, 1), :] * pltpu.roll(centre, length - 1, 1)
            return centre, total

        def force(x, y, loaded, outer):
            cell = x * wide + y
            w = (x - 1) * (breadth + 2) + y - 1
            centre, total = beside(corr, x, y)
            scale = weights[w, pl.ds(0, 1), :]
            term = scale * loaded
            if outer:
                term = jnp.where(jnp.broadcast_to(scale, term.shape) > 0, term, 0.0)
            value = term - 0.8 * centre + total
            forced[cell] = value
            first[cell] = value

        def force_row(i, carry):
            for y in range(breadth):
                start = part * own + i * breadth + y
                force(i + 2, y + 2, res[pl.ds(start, rhs, stride=parts * own), :], False)
            for side in range(2):
                start = side * rhs * parts * depth + part * depth + i
                loaded = halo_y[pl.ds(start, rhs, stride=parts * depth), :]
                force(i + 2, 1 + side * (breadth + 1), loaded, True)
            return carry

        lax.fori_loop(0, depth, force_row, 0)

        def force_edge(i, carry):
            for side in range(2):
                start = side * rhs * parts * breadth + part * breadth + i
                loaded = halo_x[pl.ds(start, rhs, stride=parts * breadth), :]
                force(1 + side * (depth + 1), i + 2, loaded, True)
            return carry

        lax.fori_loop(0, breadth, force_edge, 0)

        source, target = first, second
        for sweep in range(1, SWEEPS):
            last = sweep == SWEEPS - 1

            def relax(x, y, source=source, target=target):
                centre, total = beside(source, x, y)
                cell = x * wide + y
                target[cell] = 0.2 * centre + (forced[cell] + total)

            def finish(x, y, source=source):
                centre, total = beside(source, x, y)
                cell = x * wide + y
                value = corr[cell] + (0.2 * centre + (forced[cell] + total))
                start = part * own + (x - 2) * breadth + y - 2
                out[pl.ds(start, rhs, stride=parts * own), :] = value

            def row(i, carry, last=last, relax=relax, finish=finish):
                if last:
                    for y in range(breadth):
                        finish(i + 2, y + 2)
                else:
                    for y in range(breadth + 2):
                        relax(i + 2, y + 1)
                return carry

            lax.fori_loop(0, depth, row, 0)
            if not last:
                def edge(i, carry, relax=relax):
                    relax(1, i + 2)
                    relax(depth + 2, i + 2)
                    return carry

                lax.fori_loop(0, breadth, edge, 0)
            source, target = target, source
        return carry

    lax.fori_loop(0, parts, component, 0)


def schwarz(residuals, vectors_ext, modulus_ext, grid, halo_x, halo_y):
    rhs, parts, depth, breadth, length = residuals.shape
    width = vectors_ext.shape[0]
    diagonal, west, east, south, north, lower, upper = face_weights(modulus_ext)
    inner = modulus_ext[1:-1, 1:-1, :]
    scale = jnp.where(inner > 0, 0.8, 0.0) / diagonal
    z = jnp.arange(length, dtype=jnp.int32)
    lower = jnp.where(z > 0, lower, 0.0)
    upper = jnp.where(z < length - 1, upper, 0.0)
    weights = jnp.stack(
        [scale] + [scale * w for w in (west, east, south, north, lower, upper)] + [jnp.zeros_like(scale)],
        axis=2,
    ).reshape((depth + 2) * (breadth + 2), 8, length)
    cells = (depth + 4) * (breadth + 4)
    vec = vectors_ext.transpose(1, 2, 3, 0, 4).reshape(parts, cells, width, length)
    vmem = pl.BlockSpec(memory_space=pltpu.VMEM)
    field = pltpu.VMEM((cells, rhs, length), jnp.float32)
    result = pl.pallas_call(
        functools.partial(schwarz_kernel, rhs, parts, depth, breadth, width),
        out_shape=jax.ShapeDtypeStruct((rhs * parts * depth * breadth, length), jnp.float32),
        in_specs=[vmem] * 6,
        out_specs=vmem,
        scratch_shapes=[pltpu.VMEM((9 * width, rhs, length), jnp.float32), field, field, field, field],
        compiler_params=pltpu.CompilerParams(vmem_limit_bytes=48 * 1024 * 1024),
    )(
        residuals.reshape(-1, length),
        vec,
        weights,
        grid.T,
        halo_x.reshape(-1, length),
        halo_y.reshape(-1, length),
    )
    return result.reshape(residuals.shape)


def on_device(residuals, vectors, phases, stiffness):
    count_x = lax.axis_size("gx")
    count_y = lax.axis_size("yz")
    position = lax.axis_index("gx") * count_y + lax.axis_index("yz")
    width = vectors.shape[0]
    levels = stiffness.shape[0]
    choose = (phases[None] == jnp.arange(levels, dtype=jnp.int32)[:, None, None, None]).astype(
        jnp.float32
    )
    modulus = jnp.sum(stiffness[:, None, None, None] * choose, axis=0)
    vectors_ext = extended(vectors, (("gx", 2), ("yz", 3)), 2)
    modulus_ext = extended(modulus[None, None], (("gx", 2), ("yz", 3)), 2)[0, 0]
    blocks = coarse_blocks(vectors_ext, modulus_ext)
    coarse_rhs = jnp.einsum("kcxyz,rcxyz->kr", vectors, residuals, precision=HIGH)
    panel = panel_row(blocks, coarse_rhs, count_y)
    coeffs_all, grid, halo_x, halo_y = coarse_solve(panel, residuals, count_x, count_y, width)
    coeffs = grid[4 * width : 5 * width]
    result = schwarz(residuals, vectors_ext, modulus_ext, grid, halo_x, halo_y)
    return (coeffs, result)


def solution(mesh):
    return jax.shard_map(
        on_device,
        mesh=mesh,
        in_specs=(
            P(None, None, "gx", "yz", None),
            P(None, None, "gx", "yz", None),
            P("gx", "yz", None),
            P(),
        ),
        out_specs=(P(("gx", "yz"), None), P(None, None, "gx", "yz", None)),
        check_vma=False,
    )
```

```python
import functools

import jax
import jax.numpy as jnp
from jax import lax
from jax.experimental import pallas as pl
from jax.experimental.pallas import tpu as pltpu
from jax.sharding import PartitionSpec as P

SWEEPS = 4


HIGH = lax.Precision.HIGHEST


MESH = pl.DeviceIdType.MESH


def eliminate(rows, size):
    sublane = lax.broadcasted_iota(jnp.int32, rows[0].shape, 0)
    for p in range(size):
        reduced = []
        for a in rows:
            column = jnp.broadcast_to(a[:, p : p + 1], a.shape)
            pivot = a[p : p + 1, :] / column[p : p + 1, :]
            reduced.append(jnp.where(sublane == p, pivot, a - column * pivot))
        rows = reduced
    return rows


def product(a, b):
    return jnp.dot(a, b, precision=HIGH, preferred_element_type=jnp.float32)


def cyclic_solve(rows, size):
    count = len(rows)
    width = rows[0].shape[1]
    lane = lax.broadcasted_iota(jnp.int32, rows[0].shape, 1)
    is_own = lane < size
    is_low = (lane >= size) & (lane < 2 * size)
    is_high = (lane >= 2 * size) & (lane < 3 * size)
    is_rhs = lane >= 3 * size
    live = list(range(count))
    system = dict(enumerate(rows))
    levels = []
    while len(live) > 1:
        out = live[1::2]
        kept = live[0::2]
        solved = dict(zip(out, eliminate([system[i] for i in out], size)))
        fresh = {}
        for place, i in enumerate(kept):
            a = system[i]
            total = jnp.where(is_own | is_rhs, a, 0.0)
            if place > 0:
                t = product(a[:, size : 2 * size], solved[out[place - 1]])
                shifted = pltpu.roll(t, width - 2 * size, 1)
                total = total - jnp.where(is_own, shifted, jnp.where(is_low | is_rhs, t, 0.0))
            if place < len(out):
                t = product(a[:, 2 * size : 3 * size], solved[out[place]])
                shifted = pltpu.roll(t, width - size, 1)
                total = total - jnp.where(is_own, shifted, jnp.where(is_high | is_rhs, t, 0.0))
            fresh[i] = total
        levels.append((live, out, solved))
        system = fresh
        live = kept
    last = eliminate([system[live[0]]], size)[0]
    answer = {live[0]: last[:, 3 * size :]}
    for before, out, solved in reversed(levels):
        for i in out:
            a = solved[i]
            place = before.index(i)
            x = a[:, 3 * size :] - product(a[:, size : 2 * size], answer[before[place - 1]])
            if place + 1 < len(before):
                x = x - product(a[:, 2 * size : 3 * size], answer[before[place + 1]])
            answer[i] = x
    return [answer[i] for i in range(count)]


def cell_weights(ext, x, y):
    field = ext.shape[0] - 1
    m = ext[field, x, y]
    length = m.shape[1]
    z = lax.broadcasted_iota(jnp.int32, m.shape, 1)
    low = 0.5 * (m + jnp.where(z > 0, pltpu.roll(m, 1, 1), 0.0))
    high = 0.5 * (m + jnp.where(z < length - 1, pltpu.roll(m, length - 1, 1), 0.0))
    west = 0.5 * (m + ext[field, x - 1, y])
    east = 0.5 * (m + ext[field, x + 1, y])
    south = 0.5 * (m + ext[field, x, y - 1])
    north = 0.5 * (m + ext[field, x, y + 1])
    diagonal = 0.002 + west + east + south + north + low + high
    return m, diagonal, (
        west, east, south, north, jnp.where(z > 0, low, 0.0), jnp.where(z < length - 1, high, 0.0)
    )


def coarse_kernel(
    count_x, count_y, width, own, flat, res, south_face, north_face,
    coeffs, grid, halo_x, halo_y, ext,
    panel, gathered, send_sem, recv_sem, halo_send, halo_recv
):
    index_x = lax.axis_index("gx")
    index_y = lax.axis_index("yz")
    count = count_x * count_y
    me = index_x * count_y + index_y
    fields, depth, breadth = own.shape[:3]
    parts = fields - 1
    rhs = res.shape[0]
    length = own.shape[4]
    barrier = pltpu.get_barrier_semaphore()
    zero = jnp.zeros((width, length), jnp.float32)

    def clear(x, carry):
        for f in range(fields):
            for y in range(breadth + 4):
                ext[f, x, y] = zero
        return carry

    lax.fori_loop(0, depth + 4, clear, 0)

    def fill(x, carry):
        for f in range(fields):
            for y in range(breadth):
                ext[f, x + 2, y + 2] = own[f, x, y]
        return carry

    lax.fori_loop(0, depth, fill, 0)

    def greet(step, carry):
        other = lax.rem(me + step, count)
        pl.semaphore_signal(
            barrier, inc=1, device_id=(other // count_y, lax.rem(other, count_y)), device_id_type=MESH
        )
        return carry

    lax.fori_loop(1, count, greet, 0)
    pl.semaphore_wait(barrier, count - 1)

    def can(dx, dy):
        ok = index_x >= 0
        if dx:
            ok = index_x > 0 if dx < 0 else index_x < count_x - 1
        if dy:
            ok_y = index_y > 0 if dy < 0 else index_y < count_y - 1
            ok = jnp.logical_and(ok, ok_y) if dx else ok_y
        return ok

    started = []

    def start(source, target, dx, dy):
        slot = len(started)
        copy = pltpu.make_async_remote_copy(
            src_ref=source,
            dst_ref=target,
            send_sem=halo_send.at[slot],
            recv_sem=halo_recv.at[slot],
            device_id=(index_x + dx, index_y + dy),
            device_id_type=MESH,
        )
        pl.when(can(dx, dy))(copy.start)
        started.append((can(dx, dy), can(-dx, -dy), copy))

    def layer(step):
        inner_x, inner_y = pl.ds(2, depth), pl.ds(2, breadth)
        start(own.at[:, step], ext.at[:, depth + 2 + step, inner_y], -1, 0)
        start(own.at[:, depth - 1 - step], ext.at[:, 1 - step, inner_y], 1, 0)
        start(own.at[:, :, step], ext.at[:, inner_x, breadth + 2 + step], 0, -1)
        start(own.at[:, :, breadth - 1 - step], ext.at[:, inner_x, 1 - step], 0, 1)

    layer(0)
    cells = depth * breadth

    def loads(i, sums):
        f = i // cells
        cell = i - f * cells
        v = own[f, cell // breadth, lax.rem(cell, breadth)]
        return tuple(
            total + v * flat[pl.ds(r * parts * cells + i, 1), :] for r, total in enumerate(sums)
        )

    sums = lax.fori_loop(0, parts * cells, loads, (zero,) * rhs)
    lane = lax.broadcasted_iota(jnp.int32, panel.shape, 1)

    def placed(total, at):
        return jnp.where(lane == at, jnp.sum(total, axis=1, keepdims=True), 0.0)

    size = count_y * width
    row = jnp.zeros(panel.shape, jnp.float32)
    for r in range(rhs):
        row = row + placed(sums[r], 3 * size + r)
    for _, receives, copy in started:
        pl.when(receives)(copy.wait_recv)

    def gram(sums, left, f, x, y):
        return tuple(
            total + left * ext[f, x, y, pl.ds(l, 1), :] for l, total in enumerate(sums)
        )

    def own_block(i, sums):
        inside_x = (
            jnp.where(i > 0, 1.0, 0.0).astype(jnp.float32),
            jnp.where(i < depth - 1, 1.0, 0.0).astype(jnp.float32),
        )
        x = i + 2
        for y in range(2, breadth + 2):
            _, diagonal, (west, east, south, north, low, high) = cell_weights(ext, x, y)
            west = west * inside_x[0]
            east = east * inside_x[1]
            for f in range(parts):
                v = ext[f, x, y]
                near = west * ext[f, x - 1, y] + east * ext[f, x + 1, y]
                if y > 2:
                    near = near + south * ext[f, x, y - 1]
                if y < breadth + 1:
                    near = near + north * ext[f, x, y + 1]
                near = near + low * pltpu.roll(v, 1, 1) + high * pltpu.roll(v, length - 1, 1)
                sums = gram(sums, diagonal * v - near, f, x, y)
        return sums

    def side_block(along, fixed_x, fixed_y, dx, dy):
        which = {(-1, 0): 0, (1, 0): 1, (0, -1): 2, (0, 1): 3}[(dx, dy)]

        def one(i, sums):
            x = i + 2 if fixed_x is None else fixed_x
            y = i + 2 if fixed_y is None else fixed_y
            weight = cell_weights(ext, x, y)[2][which]
            for f in range(parts):
                sums = gram(sums, -weight * ext[f, x, y], f, x + dx, y + dy)
            return sums

        return lax.fori_loop(0, along, one, (zero,) * width)

    blocks = (
        (lax.fori_loop(0, depth, own_block, (zero,) * width), index_y * width),
        (side_block(depth, None, 2, 0, -1), (index_y - 1) * width),
        (side_block(depth, None, breadth + 1, 0, 1), (index_y + 1) * width),
        (side_block(breadth, 2, None, -1, 0), size + index_y * width),
        (side_block(breadth, depth + 1, None, 1, 0), 2 * size + index_y * width),
    )
    for totals, at in blocks:
        for l in range(width):
            row = row + placed(totals[l], at + l)
    panel[...] = row
    gathered[me] = row

    def sending(other, slot):
        return pltpu.make_async_remote_copy(
            src_ref=panel,
            dst_ref=gathered.at[slot],
            send_sem=send_sem.at[other],
            recv_sem=recv_sem.at[slot],
            device_id=(other // count_y, lax.rem(other, count_y)),
            device_id_type=MESH,
        )

    def send(step, carry):
        sending(lax.rem(me + step, count), me).start()
        return carry

    lax.fori_loop(1, count, send, 0)
    first = len(started)
    layer(1)
    ends_x = ((0, -1, depth + 2), (depth - 1, 1, 1))
    ends_y = ((0, -1, breadth + 2), (breadth - 1, 1, 1))
    for x, dx, to_x in ends_x:
        for y, dy, to_y in ends_y:
            start(own.at[:, x, y], ext.at[:, to_x, to_y], dx, dy)
    start(res.at[:, :, 0], halo_x.at[1], -1, 0)
    start(res.at[:, :, depth - 1], halo_x.at[0], 1, 0)
    start(south_face, halo_y.at[1], 0, -1)
    start(north_face, halo_y.at[0], 0, 1)

    def collect(step, carry):
        other = lax.rem(me + step, count)
        sending(other, other).wait_recv()
        return carry

    lax.fori_loop(1, count, collect, 0)
    rows = [gathered[pl.ds(g * count_y, count_y)].reshape(size, length) for g in range(count_x)]
    for g, x in enumerate(cyclic_solve(rows, size)):
        coeffs[pl.ds(g * size, size), :] = x
    slot = 0
    for step_x in (-1, 0, 1):
        for step_y in (-1, 0, 1):
            near_x = jnp.clip(index_x + step_x, 0, count_x - 1)
            near_y = jnp.clip(index_y + step_y, 0, count_y - 1)
            begin = pl.multiple_of((near_x * count_y + near_y) * width, width)
            grid[pl.ds(slot * width, width), :] = coeffs[pl.ds(begin, width), :]
            slot += 1

    def drain(step, carry):
        sending(lax.rem(me + step, count), me).wait_send()
        return carry

    lax.fori_loop(1, count, drain, 0)
    for place, (sends, receives, copy) in enumerate(started):
        pl.when(sends)(copy.wait_send)
        if place >= first:
            pl.when(receives)(copy.wait_recv)


def coarse_solve(own, residuals, count_x, count_y):
    rhs, parts, depth, breadth, length = residuals.shape
    fields, width = own.shape[0], own.shape[3]
    count = count_x * count_y
    vmem = pl.BlockSpec(memory_space=pltpu.VMEM)
    hbm = pl.BlockSpec(memory_space=pl.ANY)
    panel = (width, 3 * count_y * width + rhs)
    return pl.pallas_call(
        functools.partial(coarse_kernel, count_x, count_y, width),
        out_shape=(
            jax.ShapeDtypeStruct((count * width, rhs), jnp.float32),
            jax.ShapeDtypeStruct((9 * width, rhs), jnp.float32),
            jax.ShapeDtypeStruct((2, rhs, parts, breadth, length), jnp.float32),
            jax.ShapeDtypeStruct((2, rhs, parts, depth, length), jnp.float32),
            jax.ShapeDtypeStruct((fields, depth + 4, breadth + 4, width, length), jnp.float32),
        ),
        in_specs=[vmem, vmem, hbm, hbm, hbm],
        out_specs=(vmem, vmem, hbm, hbm, vmem),
        scratch_shapes=[
            pltpu.VMEM(panel, jnp.float32),
            pltpu.VMEM((count,) + panel, jnp.float32),
            pltpu.SemaphoreType.DMA((count,)),
            pltpu.SemaphoreType.DMA((count,)),
            pltpu.SemaphoreType.DMA((16,)),
            pltpu.SemaphoreType.DMA((16,)),
        ],
        compiler_params=pltpu.CompilerParams(collective_id=0, has_side_effects=True),
    )(
        own,
        residuals.reshape(-1, length),
        residuals,
        residuals[:, :, :, 0, :],
        residuals[:, :, :, -1, :],
    )


def schwarz_kernel(
    rhs, parts, depth, breadth, width, res, ext, cgrid, halo_x, halo_y, out,
    weights, coeff, corr, forced, first, second
):
    length = res.shape[1]
    wide = breadth + 4
    own = depth * breadth

    for cls in range(9):
        for k in range(width):
            coeff[cls * width + k] = jnp.broadcast_to(
                cgrid[:, cls * width + k : cls * width + k + 1], (rhs, length)
            )
    zero = jnp.zeros((rhs, length), jnp.float32)
    for buffer in (first, second):
        def clear(i, carry, buffer=buffer):
            buffer[i] = zero
            return carry

        lax.fori_loop(0, (depth + 4) * wide, clear, 0)

    def weigh(i, carry):
        x = i // (breadth + 2) + 1
        y = lax.rem(i, breadth + 2) + 1
        m, diagonal, faces = cell_weights(ext, x, y)
        scale = jnp.where(m > 0, 0.8, 0.0) / diagonal
        weights[i, 0] = scale
        for q, w in enumerate(faces):
            weights[i, q + 1] = scale * w
        return carry

    lax.fori_loop(0, (depth + 2) * (breadth + 2), weigh, 0)

    def spread(w, q):
        return jnp.concatenate([weights[w, q]] * (rhs // width), axis=0)

    def component(part, carry):
        def region(cls, x0, nx, y0, ny):
            def one(i, carry):
                x = x0 + i // ny
                y = y0 + lax.rem(i, ny)
                value = coeff[cls * width] * ext[part, x, y, pl.ds(0, 1), :]
                for k in range(1, width):
                    value = value + coeff[cls * width + k] * ext[part, x, y, pl.ds(k, 1), :]
                corr[x * wide + y] = value
                return carry

            lax.fori_loop(0, nx * ny, one, 0, unroll=2 if nx * ny > 1 else 1)

        spans_x = ((0, 2), (2, depth), (depth + 2, 2))
        spans_y = ((0, 2), (2, breadth), (breadth + 2, 2))
        for a, (x0, nx) in enumerate(spans_x):
            for b, (y0, ny) in enumerate(spans_y):
                if a != 1 and b != 1:
                    region(a * 3 + b, 1 if a == 0 else x0, 1, 1 if b == 0 else y0, 1)
                else:
                    region(a * 3 + b, x0, nx, y0, ny)

        def beside(buffer, x, y):
            cell = x * wide + y
            w = (x - 1) * (breadth + 2) + y - 1
            centre = buffer[cell]
            total = spread(w, 1) * buffer[cell - wide]
            total = total + spread(w, 2) * buffer[cell + wide]
            total = total + spread(w, 3) * buffer[cell - 1]
            total = total + spread(w, 4) * buffer[cell + 1]
            total = total + spread(w, 5) * pltpu.roll(centre, 1, 1)
            total = total + spread(w, 6) * pltpu.roll(centre, length - 1, 1)
            return centre, total

        def force(x, y, loaded, outer):
            cell = x * wide + y
            w = (x - 1) * (breadth + 2) + y - 1
            centre, total = beside(corr, x, y)
            scale = spread(w, 0)
            term = scale * loaded
            if outer:
                term = jnp.where(scale > 0, term, 0.0)
            value = term - 0.8 * centre + total
            forced[cell] = value
            first[cell] = value

        def force_row(i, carry):
            for y in range(breadth):
                start = part * own + i * breadth + y
                force(i + 2, y + 2, res[pl.ds(start, rhs, stride=parts * own), :], False)
            for side in range(2):
                start = side * rhs * parts * depth + part * depth + i
                loaded = halo_y[pl.ds(start, rhs, stride=parts * depth), :]
                force(i + 2, 1 + side * (breadth + 1), loaded, True)
            return carry

        lax.fori_loop(0, depth, force_row, 0)

        def force_edge(i, carry):
            for side in range(2):
                start = side * rhs * parts * breadth + part * breadth + i
                loaded = halo_x[pl.ds(start, rhs, stride=parts * breadth), :]
                force(1 + side * (depth + 1), i + 2, loaded, True)
            return carry

        lax.fori_loop(0, breadth, force_edge, 0)

        source, target = first, second
        for sweep in range(1, SWEEPS):
            last = sweep == SWEEPS - 1

            def relax(x, y, source=source, target=target):
                centre, total = beside(source, x, y)
                cell = x * wide + y
                target[cell] = 0.2 * centre + (forced[cell] + total)

            def finish(x, y, source=source):
                centre, total = beside(source, x, y)
                cell = x * wide + y
                value = corr[cell] + (0.2 * centre + (forced[cell] + total))
                start = part * own + (x - 2) * breadth + y - 2
                out[pl.ds(start, rhs, stride=parts * own), :] = value

            def row(i, carry, last=last, relax=relax, finish=finish):
                if last:
                    for y in range(breadth):
                        finish(i + 2, y + 2)
                else:
                    for y in range(breadth + 2):
                        relax(i + 2, y + 1)
                return carry

            lax.fori_loop(0, depth, row, 0)
            if not last:
                def edge(i, carry, relax=relax):
                    relax(1, i + 2)
                    relax(depth + 2, i + 2)
                    return carry

                lax.fori_loop(0, breadth, edge, 0)
            source, target = target, source
        return carry

    lax.fori_loop(0, parts, component, 0)


def schwarz(residuals, ext, grid, halo_x, halo_y):
    rhs, parts, depth, breadth, length = residuals.shape
    width = ext.shape[3]
    vmem = pl.BlockSpec(memory_space=pltpu.VMEM)
    field = pltpu.VMEM(((depth + 4) * (breadth + 4), rhs, length), jnp.float32)
    result = pl.pallas_call(
        functools.partial(schwarz_kernel, rhs, parts, depth, breadth, width),
        out_shape=jax.ShapeDtypeStruct((rhs * parts * depth * breadth, length), jnp.float32),
        in_specs=[vmem] * 5,
        out_specs=vmem,
        scratch_shapes=[
            pltpu.VMEM(((depth + 2) * (breadth + 2), 7, width, length), jnp.float32),
            pltpu.VMEM((9 * width, rhs, length), jnp.float32),
            field, field, field, field,
        ],
        compiler_params=pltpu.CompilerParams(vmem_limit_bytes=48 * 1024 * 1024),
    )(
        residuals.reshape(-1, length),
        ext,
        grid.T,
        halo_x.reshape(-1, length),
        halo_y.reshape(-1, length),
    )
    return result.reshape(residuals.shape)


def on_device(residuals, vectors, phases, stiffness):
    count_x = lax.axis_size("gx")
    count_y = lax.axis_size("yz")
    width = vectors.shape[0]
    levels = stiffness.shape[0]
    choose = (phases[None] == jnp.arange(levels, dtype=jnp.int32)[:, None, None, None]).astype(
        jnp.float32
    )
    modulus = jnp.sum(stiffness[:, None, None, None] * choose, axis=0)
    spread = jnp.broadcast_to(modulus[None, :, :, None, :], (1,) + modulus.shape[:2] + (width, modulus.shape[2]))
    own = jnp.concatenate([vectors.transpose(1, 2, 3, 0, 4), spread], axis=0)
    coeffs_all, grid, halo_x, halo_y, ext = coarse_solve(own, residuals, count_x, count_y)
    coeffs = grid[4 * width : 5 * width]
    result = schwarz(residuals, ext, grid, halo_x, halo_y)
    return (coeffs, result)


def solution(mesh):
    return jax.shard_map(
        on_device,
        mesh=mesh,
        in_specs=(
            P(None, None, "gx", "yz", None),
            P(None, None, "gx", "yz", None),
            P("gx", "yz", None),
            P(),
        ),
        out_specs=(P(("gx", "yz"), None), P(None, None, "gx", "yz", None)),
        check_vma=False,
    )
```

```python
import functools

import jax
import jax.numpy as jnp
from jax import lax
from jax.experimental import pallas as pl
from jax.experimental.pallas import tpu as pltpu
from jax.sharding import PartitionSpec as P

SWEEPS = 4


HIGH = lax.Precision.HIGHEST


MESH = pl.DeviceIdType.MESH


def eliminate(rows, size):
    sublane = lax.broadcasted_iota(jnp.int32, rows[0].shape, 0)
    for p in range(size):
        reduced = []
        for a in rows:
            column = jnp.broadcast_to(a[:, p : p + 1], a.shape)
            pivot = a[p : p + 1, :] / column[p : p + 1, :]
            reduced.append(jnp.where(sublane == p, pivot, a - column * pivot))
        rows = reduced
    return rows


def product(a, b):
    return jnp.dot(a, b, precision=HIGH, preferred_element_type=jnp.float32)


def cyclic_solve(rows, size):
    count = len(rows)
    width = rows[0].shape[1]
    lane = lax.broadcasted_iota(jnp.int32, rows[0].shape, 1)
    is_own = lane < size
    is_low = (lane >= size) & (lane < 2 * size)
    is_high = (lane >= 2 * size) & (lane < 3 * size)
    is_rhs = lane >= 3 * size
    live = list(range(count))
    system = dict(enumerate(rows))
    levels = []
    while len(live) > 1:
        out = live[1::2]
        kept = live[0::2]
        solved = dict(zip(out, eliminate([system[i] for i in out], size)))
        fresh = {}
        for place, i in enumerate(kept):
            a = system[i]
            total = jnp.where(is_own | is_rhs, a, 0.0)
            if place > 0:
                t = product(a[:, size : 2 * size], solved[out[place - 1]])
                shifted = pltpu.roll(t, width - 2 * size, 1)
                total = total - jnp.where(is_own, shifted, jnp.where(is_low | is_rhs, t, 0.0))
            if place < len(out):
                t = product(a[:, 2 * size : 3 * size], solved[out[place]])
                shifted = pltpu.roll(t, width - size, 1)
                total = total - jnp.where(is_own, shifted, jnp.where(is_high | is_rhs, t, 0.0))
            fresh[i] = total
        levels.append((live, out, solved))
        system = fresh
        live = kept
    last = eliminate([system[live[0]]], size)[0]
    answer = {live[0]: last[:, 3 * size :]}
    for before, out, solved in reversed(levels):
        for i in out:
            a = solved[i]
            place = before.index(i)
            x = a[:, 3 * size :] - product(a[:, size : 2 * size], answer[before[place - 1]])
            if place + 1 < len(before):
                x = x - product(a[:, 2 * size : 3 * size], answer[before[place + 1]])
            answer[i] = x
    return [answer[i] for i in range(count)]


def cell_weights(ext, x, y):
    field = ext.shape[0] - 1
    m = ext[field, x, y]
    length = m.shape[1]
    z = lax.broadcasted_iota(jnp.int32, m.shape, 1)
    low = 0.5 * (m + jnp.where(z > 0, pltpu.roll(m, 1, 1), 0.0))
    high = 0.5 * (m + jnp.where(z < length - 1, pltpu.roll(m, length - 1, 1), 0.0))
    west = 0.5 * (m + ext[field, x - 1, y])
    east = 0.5 * (m + ext[field, x + 1, y])
    south = 0.5 * (m + ext[field, x, y - 1])
    north = 0.5 * (m + ext[field, x, y + 1])
    diagonal = 0.002 + west + east + south + north + low + high
    return m, diagonal, (
        west, east, south, north, jnp.where(z > 0, low, 0.0), jnp.where(z < length - 1, high, 0.0)
    )


def coarse_kernel(
    count_x, count_y, width, own, flat, res,
    coeffs, grid, halo_x, halo_y, ext,
    panel, gathered, faces, send_sem, recv_sem, halo_send, halo_recv
):
    index_x = lax.axis_index("gx")
    index_y = lax.axis_index("yz")
    count = count_x * count_y
    me = index_x * count_y + index_y
    fields, depth, breadth = own.shape[:3]
    parts = fields - 1
    rhs = res.shape[0]
    length = own.shape[4]
    barrier = pltpu.get_barrier_semaphore()
    zero = jnp.zeros((width, length), jnp.float32)

    def clear(x, carry):
        for f in range(fields):
            for y in range(breadth + 4):
                ext[f, x, y] = zero
        return carry

    lax.fori_loop(0, depth + 4, clear, 0)

    def fill(x, carry):
        for f in range(fields):
            for y in range(breadth):
                ext[f, x + 2, y + 2] = own[f, x, y]
        return carry

    lax.fori_loop(0, depth, fill, 0)

    def greet(step, carry):
        other = lax.rem(me + step, count)
        pl.semaphore_signal(
            barrier, inc=1, device_id=(other // count_y, lax.rem(other, count_y)), device_id_type=MESH
        )
        return carry

    lax.fori_loop(1, count, greet, 0)

    def cut(r, carry):
        for f in range(parts):
            base = pl.multiple_of((r * parts + f) * depth * breadth, breadth)
            for side in range(2):
                faces[side, r, f] = flat[pl.ds(base + side * (breadth - 1), depth, stride=breadth), :]
        return carry

    lax.fori_loop(0, rhs, cut, 0)
    pl.semaphore_wait(barrier, count - 1)

    def can(dx, dy):
        ok = index_x >= 0
        if dx:
            ok = index_x > 0 if dx < 0 else index_x < count_x - 1
        if dy:
            ok_y = index_y > 0 if dy < 0 else index_y < count_y - 1
            ok = jnp.logical_and(ok, ok_y) if dx else ok_y
        return ok

    started = []

    def start(source, target, dx, dy):
        slot = len(started)
        copy = pltpu.make_async_remote_copy(
            src_ref=source,
            dst_ref=target,
            send_sem=halo_send.at[slot],
            recv_sem=halo_recv.at[slot],
            device_id=(index_x + dx, index_y + dy),
            device_id_type=MESH,
        )
        pl.when(can(dx, dy))(copy.start)
        started.append((can(dx, dy), can(-dx, -dy), copy))

    def layer(step):
        inner_x, inner_y = pl.ds(2, depth), pl.ds(2, breadth)
        start(own.at[:, step], ext.at[:, depth + 2 + step, inner_y], -1, 0)
        start(own.at[:, depth - 1 - step], ext.at[:, 1 - step, inner_y], 1, 0)
        start(own.at[:, :, step], ext.at[:, inner_x, breadth + 2 + step], 0, -1)
        start(own.at[:, :, breadth - 1 - step], ext.at[:, inner_x, 1 - step], 0, 1)

    layer(0)
    cells = depth * breadth

    def loads(i, sums):
        f = i // depth
        x = i - f * depth
        base = pl.multiple_of(i * breadth, breadth)
        for y in range(breadth):
            v = own[f, x, y]
            sums = tuple(
                total + v * flat[pl.ds(base + r * parts * cells + y, 1), :]
                for r, total in enumerate(sums)
            )
        return sums

    sums = lax.fori_loop(0, parts * depth, loads, (zero,) * rhs)
    lane = lax.broadcasted_iota(jnp.int32, panel.shape, 1)

    def placed(total, at):
        return jnp.where(lane == at, jnp.sum(total, axis=1, keepdims=True), 0.0)

    size = count_y * width
    row = jnp.zeros(panel.shape, jnp.float32)
    for r in range(rhs):
        row = row + placed(sums[r], 3 * size + r)
    for _, receives, copy in started:
        pl.when(receives)(copy.wait_recv)

    def gram(sums, left, f, x, y):
        return tuple(
            total + left * ext[f, x, y, pl.ds(l, 1), :] for l, total in enumerate(sums)
        )

    def own_block(i, sums):
        inside_x = (
            jnp.where(i > 0, 1.0, 0.0).astype(jnp.float32),
            jnp.where(i < depth - 1, 1.0, 0.0).astype(jnp.float32),
        )
        x = i + 2
        for y in range(2, breadth + 2):
            _, diagonal, (west, east, south, north, low, high) = cell_weights(ext, x, y)
            west = west * inside_x[0]
            east = east * inside_x[1]
            for f in range(parts):
                v = ext[f, x, y]
                near = west * ext[f, x - 1, y] + east * ext[f, x + 1, y]
                if y > 2:
                    near = near + south * ext[f, x, y - 1]
                if y < breadth + 1:
                    near = near + north * ext[f, x, y + 1]
                near = near + low * pltpu.roll(v, 1, 1) + high * pltpu.roll(v, length - 1, 1)
                sums = gram(sums, diagonal * v - near, f, x, y)
        return sums

    def side_block(along, fixed_x, fixed_y, dx, dy):
        which = {(-1, 0): 0, (1, 0): 1, (0, -1): 2, (0, 1): 3}[(dx, dy)]

        def one(i, sums):
            x = i + 2 if fixed_x is None else fixed_x
            y = i + 2 if fixed_y is None else fixed_y
            weight = cell_weights(ext, x, y)[2][which]
            for f in range(parts):
                sums = gram(sums, -weight * ext[f, x, y], f, x + dx, y + dy)
            return sums

        return lax.fori_loop(0, along, one, (zero,) * width)

    blocks = (
        (lax.fori_loop(0, depth, own_block, (zero,) * width), index_y * width),
        (side_block(depth, None, 2, 0, -1), (index_y - 1) * width),
        (side_block(depth, None, breadth + 1, 0, 1), (index_y + 1) * width),
        (side_block(breadth, 2, None, -1, 0), size + index_y * width),
        (side_block(breadth, depth + 1, None, 1, 0), 2 * size + index_y * width),
    )
    for totals, at in blocks:
        for l in range(width):
            row = row + placed(totals[l], at + l)
    panel[...] = row
    gathered[me] = row

    def sending(other, slot):
        return pltpu.make_async_remote_copy(
            src_ref=panel,
            dst_ref=gathered.at[slot],
            send_sem=send_sem.at[other],
            recv_sem=recv_sem.at[slot],
            device_id=(other // count_y, lax.rem(other, count_y)),
            device_id_type=MESH,
        )

    def send(step, carry):
        sending(lax.rem(me + step, count), me).start()
        return carry

    lax.fori_loop(1, count, send, 0)
    first = len(started)
    layer(1)
    ends_x = ((0, -1, depth + 2), (depth - 1, 1, 1))
    ends_y = ((0, -1, breadth + 2), (breadth - 1, 1, 1))
    for x, dx, to_x in ends_x:
        for y, dy, to_y in ends_y:
            start(own.at[:, x, y], ext.at[:, to_x, to_y], dx, dy)
    start(res.at[:, :, 0], halo_x.at[1], -1, 0)
    start(res.at[:, :, depth - 1], halo_x.at[0], 1, 0)
    start(faces.at[0], halo_y.at[1], 0, -1)
    start(faces.at[1], halo_y.at[0], 0, 1)

    def collect(step, carry):
        other = lax.rem(me + step, count)
        sending(other, other).wait_recv()
        return carry

    lax.fori_loop(1, count, collect, 0)
    rows = [gathered[pl.ds(g * count_y, count_y)].reshape(size, length) for g in range(count_x)]
    for g, x in enumerate(cyclic_solve(rows, size)):
        coeffs[pl.ds(g * size, size), :] = x
    grid[...] = jnp.zeros(grid.shape, jnp.float32)
    slot = 0
    for step_x in (-1, 0, 1):
        for step_y in (-1, 0, 1):
            near_x = jnp.clip(index_x + step_x, 0, count_x - 1)
            near_y = jnp.clip(index_y + step_y, 0, count_y - 1)
            begin = pl.multiple_of((near_x * count_y + near_y) * width, width)
            grid[pl.ds(slot * width, width), pl.ds(0, rhs)] = coeffs[pl.ds(begin, width), :]
            slot += 1

    def drain(step, carry):
        sending(lax.rem(me + step, count), me).wait_send()
        return carry

    lax.fori_loop(1, count, drain, 0)
    for place, (sends, receives, copy) in enumerate(started):
        pl.when(sends)(copy.wait_send)
        if place >= first:
            pl.when(receives)(copy.wait_recv)


def coarse_solve(own, residuals, count_x, count_y):
    rhs, parts, depth, breadth, length = residuals.shape
    fields, width = own.shape[0], own.shape[3]
    count = count_x * count_y
    vmem = pl.BlockSpec(memory_space=pltpu.VMEM)
    hbm = pl.BlockSpec(memory_space=pl.ANY)
    panel = (width, 3 * count_y * width + rhs)
    return pl.pallas_call(
        functools.partial(coarse_kernel, count_x, count_y, width),
        out_shape=(
            jax.ShapeDtypeStruct((count * width, rhs), jnp.float32),
            jax.ShapeDtypeStruct((pl.cdiv(9 * width, 128) * 128, pl.cdiv(rhs, 128) * 128), jnp.float32),
            jax.ShapeDtypeStruct((2, rhs, parts, breadth, length), jnp.float32),
            jax.ShapeDtypeStruct((2, rhs, parts, depth, length), jnp.float32),
            jax.ShapeDtypeStruct((fields, depth + 4, breadth + 4, width, length), jnp.float32),
        ),
        in_specs=[vmem, vmem, hbm],
        out_specs=(vmem, vmem, hbm, hbm, vmem),
        scratch_shapes=[
            pltpu.VMEM(panel, jnp.float32),
            pltpu.VMEM((count,) + panel, jnp.float32),
            pltpu.VMEM((2, rhs, parts, depth, length), jnp.float32),
            pltpu.SemaphoreType.DMA((count,)),
            pltpu.SemaphoreType.DMA((count,)),
            pltpu.SemaphoreType.DMA((16,)),
            pltpu.SemaphoreType.DMA((16,)),
        ],
        compiler_params=pltpu.CompilerParams(collective_id=0, has_side_effects=True),
    )(
        own,
        residuals.reshape(-1, length),
        residuals,
    )


def schwarz_kernel(
    rhs, parts, depth, breadth, width, res, ext, cgrid, halo_x, halo_y, out, mine,
    weights, coeff, corr, forced, first, second
):
    length = res.shape[1]
    wide = breadth + 4
    own = depth * breadth

    mine[...] = cgrid[pl.ds(4 * width, width), pl.ds(0, rhs)]
    turned = cgrid[...].T
    for i in range(9 * width):
        coeff[i] = jnp.broadcast_to(turned[:rhs, i : i + 1], (rhs, length))
    zero = jnp.zeros((rhs, length), jnp.float32)
    for buffer in (forced, first, second):
        def clear_x(y, carry, buffer=buffer):
            buffer[y] = zero
            buffer[(depth + 3) * wide + y] = zero
            return carry

        def clear_y(x, carry, buffer=buffer):
            buffer[x * wide] = zero
            buffer[x * wide + wide - 1] = zero
            return carry

        lax.fori_loop(0, wide, clear_x, 0)
        lax.fori_loop(0, depth + 4, clear_y, 0)
        for x in (1, depth + 2):
            for y in (1, breadth + 2):
                buffer[x * wide + y] = zero

    def weigh(i, carry):
        for y in range(breadth + 2):
            m, diagonal, faces = cell_weights(ext, i + 1, y + 1)
            scale = jnp.where(m > 0, 0.8, 0.0) / diagonal
            at = i * (breadth + 2) + y
            weights[at, 0] = scale
            for q, w in enumerate(faces):
                weights[at, q + 1] = scale * w
        return carry

    lax.fori_loop(0, depth + 2, weigh, 0)

    def spread(w, q):
        return jnp.concatenate([weights[w, q]] * (rhs // width), axis=0)

    def component(part, carry):
        def correct(cls, cells):
            values = [None] * len(cells)
            for k in range(width):
                c = coeff[cls * width + k]
                for i, (x, y) in enumerate(cells):
                    term = c * ext[part, x, y, pl.ds(k, 1), :]
                    values[i] = term if k == 0 else values[i] + term
            for (x, y), value in zip(cells, values):
                corr[x * wide + y] = value

        def along_y(cls, x0, nx):
            def one(i, carry):
                correct(cls, [(x0 + i, y + 2) for y in range(breadth)])
                return carry

            lax.fori_loop(0, nx, one, 0)

        def along_x(cls, y0):
            def one(i, carry):
                correct(cls, [(x + 2, y0 + i) for x in range(depth)])
                return carry

            lax.fori_loop(0, 2, one, 0)

        along_y(4, 2, depth)
        along_y(1, 0, 2)
        along_y(7, depth + 2, 2)
        along_x(3, 0)
        along_x(5, breadth + 2)
        for cls, x, y in (
            (0, 1, 1), (2, 1, breadth + 2), (6, depth + 2, 1), (8, depth + 2, breadth + 2)
        ):
            correct(cls, [(x, y)])

        def beside(buffer, x, y):
            cell = x * wide + y
            w = (x - 1) * (breadth + 2) + y - 1
            centre = buffer[cell]
            total = spread(w, 1) * buffer[cell - wide]
            total = total + spread(w, 2) * buffer[cell + wide]
            total = total + spread(w, 3) * buffer[cell - 1]
            total = total + spread(w, 4) * buffer[cell + 1]
            total = total + spread(w, 5) * pltpu.roll(centre, 1, 1)
            total = total + spread(w, 6) * pltpu.roll(centre, length - 1, 1)
            return centre, total

        def force(x, y, loaded, outer):
            cell = x * wide + y
            w = (x - 1) * (breadth + 2) + y - 1
            centre, total = beside(corr, x, y)
            scale = spread(w, 0)
            term = scale * loaded
            if outer:
                term = jnp.where(scale > 0, term, 0.0)
            forced[cell] = term - 0.8 * centre + total

        def force_row(i, carry):
            for y in range(breadth):
                start = part * own + i * breadth + y
                force(i + 2, y + 2, res[pl.ds(start, rhs, stride=parts * own), :], False)
            for side in range(2):
                start = side * rhs * parts * depth + part * depth + i
                loaded = halo_y[pl.ds(start, rhs, stride=parts * depth), :]
                force(i + 2, 1 + side * (breadth + 1), loaded, True)
            return carry

        lax.fori_loop(0, depth, force_row, 0)

        def force_edge(i, carry):
            for side in range(2):
                start = side * rhs * parts * breadth + part * breadth + i
                loaded = halo_x[pl.ds(start, rhs, stride=parts * breadth), :]
                force(1 + side * (depth + 1), i + 2, loaded, True)
            return carry

        lax.fori_loop(0, breadth, force_edge, 0)

        source, target, spare = forced, first, second
        for sweep in range(1, SWEEPS):
            last = sweep == SWEEPS - 1

            def relaxed(x, y, source=source, opening=sweep == 1):
                centre, total = beside(source, x, y)
                if opening:
                    return 1.2 * centre + total
                return 0.2 * centre + (forced[x * wide + y] + total)

            def relax(x, y, target=target, relaxed=relaxed):
                target[x * wide + y] = relaxed(x, y)

            def finish(x, y, relaxed=relaxed):
                value = corr[x * wide + y] + relaxed(x, y)
                start = part * own + (x - 2) * breadth + y - 2
                out[pl.ds(start, rhs, stride=parts * own), :] = value

            def row(i, carry, last=last, relax=relax, finish=finish):
                if last:
                    for y in range(breadth):
                        finish(i + 2, y + 2)
                else:
                    for y in range(breadth + 2):
                        relax(i + 2, y + 1)
                return carry

            lax.fori_loop(0, depth, row, 0)
            if not last:
                def edge(i, carry, relax=relax):
                    relax(1, i + 2)
                    relax(depth + 2, i + 2)
                    return carry

                lax.fori_loop(0, breadth, edge, 0)
            source, target, spare = target, spare, target
        return carry

    lax.fori_loop(0, parts, component, 0)


def schwarz(residuals, ext, grid, halo_x, halo_y):
    rhs, parts, depth, breadth, length = residuals.shape
    width = ext.shape[3]
    vmem = pl.BlockSpec(memory_space=pltpu.VMEM)
    field = pltpu.VMEM(((depth + 4) * (breadth + 4), rhs, length), jnp.float32)
    result, coeffs = pl.pallas_call(
        functools.partial(schwarz_kernel, rhs, parts, depth, breadth, width),
        out_shape=(
            jax.ShapeDtypeStruct((rhs * parts * depth * breadth, length), jnp.float32),
            jax.ShapeDtypeStruct((width, rhs), jnp.float32),
        ),
        in_specs=[vmem] * 5,
        out_specs=(vmem, vmem),
        scratch_shapes=[
            pltpu.VMEM(((depth + 2) * (breadth + 2), 7, width, length), jnp.float32),
            pltpu.VMEM((9 * width, rhs, length), jnp.float32),
            field, field, field, field,
        ],
        compiler_params=pltpu.CompilerParams(vmem_limit_bytes=48 * 1024 * 1024),
    )(
        residuals.reshape(-1, length),
        ext,
        grid,
        halo_x.reshape(-1, length),
        halo_y.reshape(-1, length),
    )
    return coeffs, result.reshape(residuals.shape)


def on_device(residuals, vectors, phases, stiffness):
    count_x = lax.axis_size("gx")
    count_y = lax.axis_size("yz")
    width = vectors.shape[0]
    levels = stiffness.shape[0]
    choose = (phases[None] == jnp.arange(levels, dtype=jnp.int32)[:, None, None, None]).astype(
        jnp.float32
    )
    modulus = jnp.sum(stiffness[:, None, None, None] * choose, axis=0)
    spread = jnp.broadcast_to(modulus[None, :, :, None, :], (1,) + modulus.shape[:2] + (width, modulus.shape[2]))
    own = jnp.concatenate([vectors.transpose(1, 2, 3, 0, 4), spread], axis=0)
    _, grid, halo_x, halo_y, ext = coarse_solve(own, residuals, count_x, count_y)
    return schwarz(residuals, ext, grid, halo_x, halo_y)


def solution(mesh):
    return jax.shard_map(
        on_device,
        mesh=mesh,
        in_specs=(
            P(None, None, "gx", "yz", None),
            P(None, None, "gx", "yz", None),
            P("gx", "yz", None),
            P(),
        ),
        out_specs=(P(("gx", "yz"), None), P(None, None, "gx", "yz", None)),
        check_vma=False,
    )
```

```python
import functools

import jax
import jax.numpy as jnp
from jax import lax
from jax.experimental import pallas as pl
from jax.experimental.pallas import tpu as pltpu
from jax.sharding import PartitionSpec as P

SWEEPS = 4


HIGH = lax.Precision.HIGHEST


MESH = pl.DeviceIdType.MESH


def eliminate(rows, size):
    sublane = lax.broadcasted_iota(jnp.int32, rows[0].shape, 0)
    for p in range(size):
        reduced = []
        for a in rows:
            column = jnp.broadcast_to(a[:, p : p + 1], a.shape)
            pivot = a[p : p + 1, :] / column[p : p + 1, :]
            reduced.append(jnp.where(sublane == p, pivot, a - column * pivot))
        rows = reduced
    return rows


def product(a, b):
    return jnp.dot(a, b, precision=HIGH, preferred_element_type=jnp.float32)


def cyclic_solve(rows, size):
    count = len(rows)
    width = rows[0].shape[1]
    lane = lax.broadcasted_iota(jnp.int32, rows[0].shape, 1)
    is_own = lane < size
    is_low = (lane >= size) & (lane < 2 * size)
    is_high = (lane >= 2 * size) & (lane < 3 * size)
    is_rhs = lane >= 3 * size
    live = list(range(count))
    system = dict(enumerate(rows))
    levels = []
    while len(live) > 1:
        out = live[1::2]
        kept = live[0::2]
        solved = dict(zip(out, eliminate([system[i] for i in out], size)))
        fresh = {}
        for place, i in enumerate(kept):
            a = system[i]
            total = jnp.where(is_own | is_rhs, a, 0.0)
            if place > 0:
                t = product(a[:, size : 2 * size], solved[out[place - 1]])
                shifted = pltpu.roll(t, width - 2 * size, 1)
                total = total - jnp.where(is_own, shifted, jnp.where(is_low | is_rhs, t, 0.0))
            if place < len(out):
                t = product(a[:, 2 * size : 3 * size], solved[out[place]])
                shifted = pltpu.roll(t, width - size, 1)
                total = total - jnp.where(is_own, shifted, jnp.where(is_high | is_rhs, t, 0.0))
            fresh[i] = total
        levels.append((live, out, solved))
        system = fresh
        live = kept
    last = eliminate([system[live[0]]], size)[0]
    answer = {live[0]: last[:, 3 * size :]}
    for before, out, solved in reversed(levels):
        for i in out:
            a = solved[i]
            place = before.index(i)
            x = a[:, 3 * size :] - product(a[:, size : 2 * size], answer[before[place - 1]])
            if place + 1 < len(before):
                x = x - product(a[:, 2 * size : 3 * size], answer[before[place + 1]])
            answer[i] = x
    return [answer[i] for i in range(count)]


def cell_weights(ext, x, y):
    field = ext.shape[0] - 1
    m = ext[field, x, y]
    length = m.shape[1]
    z = lax.broadcasted_iota(jnp.int32, m.shape, 1)
    low = 0.5 * (m + jnp.where(z > 0, pltpu.roll(m, 1, 1), 0.0))
    high = 0.5 * (m + jnp.where(z < length - 1, pltpu.roll(m, length - 1, 1), 0.0))
    west = 0.5 * (m + ext[field, x - 1, y])
    east = 0.5 * (m + ext[field, x + 1, y])
    south = 0.5 * (m + ext[field, x, y - 1])
    north = 0.5 * (m + ext[field, x, y + 1])
    diagonal = 0.002 + west + east + south + north + low + high
    return m, diagonal, (
        west, east, south, north, jnp.where(z > 0, low, 0.0), jnp.where(z < length - 1, high, 0.0)
    )


def coarse_kernel(
    count_x, count_y, width, own, flat, res,
    coeffs, grid, halo_x, halo_y, ext,
    panel, gathered, faces, send_sem, recv_sem, halo_send, halo_recv
):
    index_x = lax.axis_index("gx")
    index_y = lax.axis_index("yz")
    count = count_x * count_y
    me = index_x * count_y + index_y
    fields, depth, breadth = own.shape[:3]
    parts = fields - 1
    rhs = res.shape[0]
    length = own.shape[4]
    barrier = pltpu.get_barrier_semaphore()
    zero = jnp.zeros((width, length), jnp.float32)

    def clear(x, carry):
        for f in range(fields):
            for y in range(breadth + 4):
                ext[f, x, y] = zero
        return carry

    lax.fori_loop(0, depth + 4, clear, 0)

    def greet(step, carry):
        other = lax.rem(me + step, count)
        pl.semaphore_signal(
            barrier, inc=1, device_id=(other // count_y, lax.rem(other, count_y)), device_id_type=MESH
        )
        return carry

    lax.fori_loop(1, count, greet, 0)

    def cut(r, carry):
        for f in range(parts):
            base = pl.multiple_of((r * parts + f) * depth * breadth, breadth)
            for side in range(2):
                faces[side, r, f] = flat[pl.ds(base + side * (breadth - 1), depth, stride=breadth), :]
        return carry

    lax.fori_loop(0, rhs, cut, 0)
    pl.semaphore_wait(barrier, count - 1)

    def can(dx, dy):
        ok = index_x >= 0
        if dx:
            ok = index_x > 0 if dx < 0 else index_x < count_x - 1
        if dy:
            ok_y = index_y > 0 if dy < 0 else index_y < count_y - 1
            ok = jnp.logical_and(ok, ok_y) if dx else ok_y
        return ok

    started = []

    def start(source, target, dx, dy):
        slot = len(started)
        copy = pltpu.make_async_remote_copy(
            src_ref=source,
            dst_ref=target,
            send_sem=halo_send.at[slot],
            recv_sem=halo_recv.at[slot],
            device_id=(index_x + dx, index_y + dy),
            device_id_type=MESH,
        )
        pl.when(can(dx, dy))(copy.start)
        started.append((can(dx, dy), can(-dx, -dy), copy))

    def layer(step):
        inner_x, inner_y = pl.ds(2, depth), pl.ds(2, breadth)
        start(own.at[:, step], ext.at[:, depth + 2 + step, inner_y], -1, 0)
        start(own.at[:, depth - 1 - step], ext.at[:, 1 - step, inner_y], 1, 0)
        start(own.at[:, :, step], ext.at[:, inner_x, breadth + 2 + step], 0, -1)
        start(own.at[:, :, breadth - 1 - step], ext.at[:, inner_x, 1 - step], 0, 1)

    def rows(low, count):
        part = pl.ds(low, count)
        start(res.at[part, :, 0], halo_x.at[1, part], -1, 0)
        start(res.at[part, :, depth - 1], halo_x.at[0, part], 1, 0)

    early = rhs * 3 // 8
    layer(0)
    first = len(started)
    rows(0, early)
    def fill(x, carry):
        for f in range(fields):
            for y in range(breadth):
                ext[f, x + 2, y + 2] = own[f, x, y]
        return carry

    lax.fori_loop(0, depth, fill, 0)

    cells = depth * breadth

    def loads(i, sums):
        f = i // depth
        x = i - f * depth
        base = pl.multiple_of(i * breadth, breadth)
        for y in range(breadth):
            v = own[f, x, y]
            sums = tuple(
                total + v * flat[pl.ds(base + r * parts * cells + y, 1), :]
                for r, total in enumerate(sums)
            )
        return sums

    sums = lax.fori_loop(0, parts * depth, loads, (zero,) * rhs)
    lane = lax.broadcasted_iota(jnp.int32, panel.shape, 1)

    def placed(total, at):
        return jnp.where(lane == at, jnp.sum(total, axis=1, keepdims=True), 0.0)

    size = count_y * width
    row = jnp.zeros(panel.shape, jnp.float32)
    for r in range(rhs):
        row = row + placed(sums[r], 3 * size + r)
    for _, receives, copy in started[:first]:
        pl.when(receives)(copy.wait_recv)

    def gram(sums, left, f, x, y):
        return tuple(
            total + left * ext[f, x, y, pl.ds(l, 1), :] for l, total in enumerate(sums)
        )

    def own_block(i, sums):
        inside_x = (
            jnp.where(i > 0, 1.0, 0.0).astype(jnp.float32),
            jnp.where(i < depth - 1, 1.0, 0.0).astype(jnp.float32),
        )
        x = i + 2
        for y in range(2, breadth + 2):
            _, diagonal, (west, east, south, north, low, high) = cell_weights(ext, x, y)
            west = west * inside_x[0]
            east = east * inside_x[1]
            for f in range(parts):
                v = ext[f, x, y]
                near = west * ext[f, x - 1, y] + east * ext[f, x + 1, y]
                if y > 2:
                    near = near + south * ext[f, x, y - 1]
                if y < breadth + 1:
                    near = near + north * ext[f, x, y + 1]
                near = near + low * pltpu.roll(v, 1, 1) + high * pltpu.roll(v, length - 1, 1)
                sums = gram(sums, diagonal * v - near, f, x, y)
        return sums

    def side_block(along, fixed_x, fixed_y, dx, dy):
        which = {(-1, 0): 0, (1, 0): 1, (0, -1): 2, (0, 1): 3}[(dx, dy)]

        def one(i, sums):
            x = i + 2 if fixed_x is None else fixed_x
            y = i + 2 if fixed_y is None else fixed_y
            weight = cell_weights(ext, x, y)[2][which]
            for f in range(parts):
                sums = gram(sums, -weight * ext[f, x, y], f, x + dx, y + dy)
            return sums

        return lax.fori_loop(0, along, one, (zero,) * width)

    blocks = (
        (lax.fori_loop(0, depth, own_block, (zero,) * width), index_y * width),
        (side_block(depth, None, 2, 0, -1), (index_y - 1) * width),
        (side_block(depth, None, breadth + 1, 0, 1), (index_y + 1) * width),
        (side_block(breadth, 2, None, -1, 0), size + index_y * width),
        (side_block(breadth, depth + 1, None, 1, 0), 2 * size + index_y * width),
    )
    for totals, at in blocks:
        for l in range(width):
            row = row + placed(totals[l], at + l)
    panel[...] = row
    gathered[me] = row

    def sending(other, slot):
        return pltpu.make_async_remote_copy(
            src_ref=panel,
            dst_ref=gathered.at[slot],
            send_sem=send_sem.at[other],
            recv_sem=recv_sem.at[slot],
            device_id=(other // count_y, lax.rem(other, count_y)),
            device_id_type=MESH,
        )

    def send(step, carry):
        sending(lax.rem(me + step, count), me).start()
        return carry

    lax.fori_loop(1, count, send, 0)
    rows(early, rhs - early)
    layer(1)
    ends_x = ((0, -1, depth + 2), (depth - 1, 1, 1))
    ends_y = ((0, -1, breadth + 2), (breadth - 1, 1, 1))
    for x, dx, to_x in ends_x:
        for y, dy, to_y in ends_y:
            start(own.at[:, x, y], ext.at[:, to_x, to_y], dx, dy)
    start(faces.at[0], halo_y.at[1], 0, -1)
    start(faces.at[1], halo_y.at[0], 0, 1)

    def collect(step, carry):
        other = lax.rem(me + step, count)
        sending(other, other).wait_recv()
        return carry

    lax.fori_loop(1, count, collect, 0)
    panels = [gathered[pl.ds(g * count_y, count_y)].reshape(size, length) for g in range(count_x)]
    for g, x in enumerate(cyclic_solve(panels, size)):
        coeffs[pl.ds(g * size, size), :] = x
    grid[...] = jnp.zeros(grid.shape, jnp.float32)
    slot = 0
    for step_x in (-1, 0, 1):
        for step_y in (-1, 0, 1):
            near_x = jnp.clip(index_x + step_x, 0, count_x - 1)
            near_y = jnp.clip(index_y + step_y, 0, count_y - 1)
            begin = pl.multiple_of((near_x * count_y + near_y) * width, width)
            grid[pl.ds(slot * width, width), pl.ds(0, rhs)] = coeffs[pl.ds(begin, width), :]
            slot += 1

    def drain(step, carry):
        sending(lax.rem(me + step, count), me).wait_send()
        return carry

    lax.fori_loop(1, count, drain, 0)
    for place, (sends, receives, copy) in enumerate(started):
        pl.when(sends)(copy.wait_send)
        if place >= first:
            pl.when(receives)(copy.wait_recv)


def coarse_solve(own, residuals, count_x, count_y):
    rhs, parts, depth, breadth, length = residuals.shape
    fields, width = own.shape[0], own.shape[3]
    count = count_x * count_y
    vmem = pl.BlockSpec(memory_space=pltpu.VMEM)
    hbm = pl.BlockSpec(memory_space=pl.ANY)
    panel = (width, 3 * count_y * width + rhs)
    return pl.pallas_call(
        functools.partial(coarse_kernel, count_x, count_y, width),
        out_shape=(
            jax.ShapeDtypeStruct((count * width, rhs), jnp.float32),
            jax.ShapeDtypeStruct((pl.cdiv(9 * width, 128) * 128, pl.cdiv(rhs, 128) * 128), jnp.float32),
            jax.ShapeDtypeStruct((2, rhs, parts, breadth, length), jnp.float32),
            jax.ShapeDtypeStruct((2, rhs, parts, depth, length), jnp.float32),
            jax.ShapeDtypeStruct((fields, depth + 4, breadth + 4, width, length), jnp.float32),
        ),
        in_specs=[vmem, vmem, hbm],
        out_specs=(vmem, vmem, hbm, hbm, vmem),
        scratch_shapes=[
            pltpu.VMEM(panel, jnp.float32),
            pltpu.VMEM((count,) + panel, jnp.float32),
            pltpu.VMEM((2, rhs, parts, depth, length), jnp.float32),
            pltpu.SemaphoreType.DMA((count,)),
            pltpu.SemaphoreType.DMA((count,)),
            pltpu.SemaphoreType.DMA((18,)),
            pltpu.SemaphoreType.DMA((18,)),
        ],
        compiler_params=pltpu.CompilerParams(collective_id=0, has_side_effects=True),
    )(
        own,
        residuals.reshape(-1, length),
        residuals,
    )


def schwarz_kernel(
    rhs, parts, depth, breadth, width, res_any, ext_any, cgrid, halo_x_any, halo_y_any, out_any, mine,
    res, ext, halo_x, halo_y, out, load_sem, ext_sem, out_sem,
    weights, coeff, corr, forced, first, second
):
    length = res.shape[1]
    wide = breadth + 4

    def load_field(f):
        return pltpu.make_async_copy(ext_any.at[f], ext.at[f], ext_sem.at[f])

    loads = [
        pltpu.make_async_copy(source, target, load_sem.at[i])
        for i, (source, target) in enumerate(((res_any, res), (halo_x_any, halo_x), (halo_y_any, halo_y)))
    ]
    for f in (parts, *range(parts)):
        load_field(f).start()
    for copy in loads:
        copy.start()
    own = depth * breadth

    mine[...] = cgrid[pl.ds(4 * width, width), pl.ds(0, rhs)]
    turned = cgrid[...].T
    for i in range(9 * width):
        coeff[i] = jnp.broadcast_to(turned[:rhs, i : i + 1], (rhs, length))
    zero = jnp.zeros((rhs, length), jnp.float32)
    for buffer in (forced, first, second):
        def clear_x(y, carry, buffer=buffer):
            buffer[y] = zero
            buffer[(depth + 3) * wide + y] = zero
            return carry

        def clear_y(x, carry, buffer=buffer):
            buffer[x * wide] = zero
            buffer[x * wide + wide - 1] = zero
            return carry

        lax.fori_loop(0, wide, clear_x, 0)
        lax.fori_loop(0, depth + 4, clear_y, 0)
        for x in (1, depth + 2):
            for y in (1, breadth + 2):
                buffer[x * wide + y] = zero

    load_field(parts).wait()

    def weigh(i, carry):
        for y in range(breadth + 2):
            m, diagonal, faces = cell_weights(ext, i + 1, y + 1)
            scale = jnp.where(m > 0, 0.8, 0.0) / diagonal
            at = i * (breadth + 2) + y
            weights[at, 0] = scale
            for q, w in enumerate(faces):
                weights[at, q + 1] = scale * w
        return carry

    lax.fori_loop(0, depth + 2, weigh, 0)

    def spread(w, q):
        return jnp.concatenate([weights[w, q]] * (rhs // width), axis=0)

    def component(part, carry):
        load_field(part).wait()

        def correct(cls, cells):
            values = [None] * len(cells)
            for k in range(width):
                c = coeff[cls * width + k]
                for i, (x, y) in enumerate(cells):
                    term = c * ext[part, x, y, pl.ds(k, 1), :]
                    values[i] = term if k == 0 else values[i] + term
            for (x, y), value in zip(cells, values):
                corr[x * wide + y] = value

        def along_y(cls, x0, nx):
            def one(i, carry):
                correct(cls, [(x0 + i, y + 2) for y in range(breadth)])
                return carry

            lax.fori_loop(0, nx, one, 0)

        def along_x(cls, y0):
            def one(i, carry):
                correct(cls, [(x + 2, y0 + i) for x in range(depth)])
                return carry

            lax.fori_loop(0, 2, one, 0)

        along_y(4, 2, depth)
        along_y(1, 0, 2)
        along_y(7, depth + 2, 2)
        along_x(3, 0)
        along_x(5, breadth + 2)
        for cls, x, y in (
            (0, 1, 1), (2, 1, breadth + 2), (6, depth + 2, 1), (8, depth + 2, breadth + 2)
        ):
            correct(cls, [(x, y)])

        def beside(buffer, x, y):
            cell = x * wide + y
            w = (x - 1) * (breadth + 2) + y - 1
            centre = buffer[cell]
            total = spread(w, 1) * buffer[cell - wide]
            total = total + spread(w, 2) * buffer[cell + wide]
            total = total + spread(w, 3) * buffer[cell - 1]
            total = total + spread(w, 4) * buffer[cell + 1]
            total = total + spread(w, 5) * pltpu.roll(centre, 1, 1)
            total = total + spread(w, 6) * pltpu.roll(centre, length - 1, 1)
            return centre, total

        def force(x, y, loaded, outer):
            cell = x * wide + y
            w = (x - 1) * (breadth + 2) + y - 1
            centre, total = beside(corr, x, y)
            scale = spread(w, 0)
            term = scale * loaded
            if outer:
                term = jnp.where(scale > 0, term, 0.0)
            forced[cell] = term - 0.8 * centre + total

        def force_row(i, carry):
            for y in range(breadth):
                start = part * own + i * breadth + y
                force(i + 2, y + 2, res[pl.ds(start, rhs, stride=parts * own), :], False)
            for side in range(2):
                start = side * rhs * parts * depth + part * depth + i
                loaded = halo_y[pl.ds(start, rhs, stride=parts * depth), :]
                force(i + 2, 1 + side * (breadth + 1), loaded, True)
            return carry

        @pl.when(part == 0)
        def _():
            for copy in loads:
                copy.wait()

        lax.fori_loop(0, depth, force_row, 0)

        def force_edge(i, carry):
            for side in range(2):
                start = side * rhs * parts * breadth + part * breadth + i
                loaded = halo_x[pl.ds(start, rhs, stride=parts * breadth), :]
                force(1 + side * (depth + 1), i + 2, loaded, True)
            return carry

        lax.fori_loop(0, breadth, force_edge, 0)

        source, target, spare = forced, first, second
        for sweep in range(1, SWEEPS):
            last = sweep == SWEEPS - 1

            def relaxed(x, y, source=source, opening=sweep == 1):
                centre, total = beside(source, x, y)
                if opening:
                    return 1.2 * centre + total
                return 0.2 * centre + (forced[x * wide + y] + total)

            def relax(x, y, target=target, relaxed=relaxed):
                target[x * wide + y] = relaxed(x, y)

            def finish(x, y, relaxed=relaxed):
                value = corr[x * wide + y] + relaxed(x, y)
                start = part * rhs * own + (x - 2) * breadth + y - 2
                out[pl.ds(start, rhs, stride=own), :] = value

            def row(i, carry, last=last, relax=relax, finish=finish):
                if last:
                    for y in range(breadth):
                        finish(i + 2, y + 2)
                else:
                    for y in range(breadth + 2):
                        relax(i + 2, y + 1)
                return carry

            lax.fori_loop(0, depth, row, 0)
            if not last:
                def edge(i, carry, relax=relax):
                    relax(1, i + 2)
                    relax(depth + 2, i + 2)
                    return carry

                lax.fori_loop(0, breadth, edge, 0)
            source, target, spare = target, spare, target

        def write(r, carry):
            pltpu.make_async_copy(
                out.at[pl.ds(pl.multiple_of((part * rhs + r) * own, own), own)],
                out_any.at[pl.ds(pl.multiple_of((r * parts + part) * own, own), own)],
                out_sem,
            ).start()
            return carry

        lax.fori_loop(0, rhs, write, 0)
        return carry

    lax.fori_loop(0, parts, component, 0)
    pltpu.make_async_copy(out, out_any, out_sem).wait()


def schwarz(residuals, ext, grid, halo_x, halo_y):
    rhs, parts, depth, breadth, length = residuals.shape
    width = ext.shape[3]
    vmem = pl.BlockSpec(memory_space=pltpu.VMEM)
    hbm = pl.BlockSpec(memory_space=pl.ANY)
    field = pltpu.VMEM(((depth + 4) * (breadth + 4), rhs, length), jnp.float32)
    result, coeffs = pl.pallas_call(
        functools.partial(schwarz_kernel, rhs, parts, depth, breadth, width),
        out_shape=(
            jax.ShapeDtypeStruct((rhs * parts * depth * breadth, length), jnp.float32),
            jax.ShapeDtypeStruct((width, rhs), jnp.float32),
        ),
        in_specs=[hbm, hbm, vmem, hbm, hbm],
        out_specs=(hbm, vmem),
        scratch_shapes=[
            pltpu.VMEM((residuals.size // length, length), jnp.float32),
            pltpu.VMEM(ext.shape, jnp.float32),
            pltpu.VMEM((halo_x.size // length, length), jnp.float32),
            pltpu.VMEM((halo_y.size // length, length), jnp.float32),
            pltpu.VMEM((residuals.size // length, length), jnp.float32),
            pltpu.SemaphoreType.DMA((3,)),
            pltpu.SemaphoreType.DMA((parts + 1,)),
            pltpu.SemaphoreType.DMA,
            pltpu.VMEM(((depth + 2) * (breadth + 2), 7, width, length), jnp.float32),
            pltpu.VMEM((9 * width, rhs, length), jnp.float32),
            field, field, field, field,
        ],
        compiler_params=pltpu.CompilerParams(vmem_limit_bytes=63 * 1024 * 1024),
    )(
        residuals.reshape(-1, length),
        ext,
        grid,
        halo_x.reshape(-1, length),
        halo_y.reshape(-1, length),
    )
    return coeffs, result.reshape(residuals.shape)


def on_device(residuals, vectors, phases, stiffness):
    count_x = lax.axis_size("gx")
    count_y = lax.axis_size("yz")
    width = vectors.shape[0]
    levels = stiffness.shape[0]
    choose = (phases[None] == jnp.arange(levels, dtype=jnp.int32)[:, None, None, None]).astype(
        jnp.float32
    )
    modulus = jnp.sum(stiffness[:, None, None, None] * choose, axis=0)
    spread = jnp.broadcast_to(modulus[None, :, :, None, :], (1,) + modulus.shape[:2] + (width, modulus.shape[2]))
    own = jnp.concatenate([vectors.transpose(1, 2, 3, 0, 4), spread], axis=0)
    _, grid, halo_x, halo_y, ext = coarse_solve(own, residuals, count_x, count_y)
    return schwarz(residuals, ext, grid, halo_x, halo_y)


def solution(mesh):
    return jax.shard_map(
        on_device,
        mesh=mesh,
        in_specs=(
            P(None, None, "gx", "yz", None),
            P(None, None, "gx", "yz", None),
            P("gx", "yz", None),
            P(),
        ),
        out_specs=(P(("gx", "yz"), None), P(None, None, "gx", "yz", None)),
        check_vma=False,
    )
```

```python
import functools

import jax
import jax.numpy as jnp
from jax import lax
from jax.experimental import pallas as pl
from jax.experimental.pallas import tpu as pltpu
from jax.sharding import PartitionSpec as P

SWEEPS = 4


HIGH = lax.Precision.HIGHEST


MESH = pl.DeviceIdType.MESH


def eliminate(rows, size):
    sublane = lax.broadcasted_iota(jnp.int32, rows[0].shape, 0)
    for p in range(size):
        reduced = []
        for a in rows:
            column = jnp.broadcast_to(a[:, p : p + 1], a.shape)
            pivot = a[p : p + 1, :] / column[p : p + 1, :]
            reduced.append(jnp.where(sublane == p, pivot, a - column * pivot))
        rows = reduced
    return rows


def product(a, b):
    return jnp.dot(a, b, precision=HIGH, preferred_element_type=jnp.float32)


def cyclic_solve(rows, size):
    count = len(rows)
    width = rows[0].shape[1]
    lane = lax.broadcasted_iota(jnp.int32, rows[0].shape, 1)
    is_own = lane < size
    is_low = (lane >= size) & (lane < 2 * size)
    is_high = (lane >= 2 * size) & (lane < 3 * size)
    is_rhs = lane >= 3 * size
    live = list(range(count))
    system = dict(enumerate(rows))
    levels = []
    while len(live) > 1:
        out = live[1::2]
        kept = live[0::2]
        solved = dict(zip(out, eliminate([system[i] for i in out], size)))
        fresh = {}
        for place, i in enumerate(kept):
            a = system[i]
            total = jnp.where(is_own | is_rhs, a, 0.0)
            if place > 0:
                t = product(a[:, size : 2 * size], solved[out[place - 1]])
                shifted = pltpu.roll(t, width - 2 * size, 1)
                total = total - jnp.where(is_own, shifted, jnp.where(is_low | is_rhs, t, 0.0))
            if place < len(out):
                t = product(a[:, 2 * size : 3 * size], solved[out[place]])
                shifted = pltpu.roll(t, width - size, 1)
                total = total - jnp.where(is_own, shifted, jnp.where(is_high | is_rhs, t, 0.0))
            fresh[i] = total
        levels.append((live, out, solved))
        system = fresh
        live = kept
    last = eliminate([system[live[0]]], size)[0]
    answer = {live[0]: last[:, 3 * size :]}
    for before, out, solved in reversed(levels):
        for i in out:
            a = solved[i]
            place = before.index(i)
            x = a[:, 3 * size :] - product(a[:, size : 2 * size], answer[before[place - 1]])
            if place + 1 < len(before):
                x = x - product(a[:, 2 * size : 3 * size], answer[before[place + 1]])
            answer[i] = x
    return [answer[i] for i in range(count)]


def cell_weights(ext, x, y):
    field = ext.shape[0] - 1
    m = ext[field, x, y]
    length = m.shape[1]
    z = lax.broadcasted_iota(jnp.int32, m.shape, 1)
    low = 0.5 * (m + jnp.where(z > 0, pltpu.roll(m, 1, 1), 0.0))
    high = 0.5 * (m + jnp.where(z < length - 1, pltpu.roll(m, length - 1, 1), 0.0))
    west = 0.5 * (m + ext[field, x - 1, y])
    east = 0.5 * (m + ext[field, x + 1, y])
    south = 0.5 * (m + ext[field, x, y - 1])
    north = 0.5 * (m + ext[field, x, y + 1])
    diagonal = 0.002 + west + east + south + north + low + high
    return m, diagonal, (
        west, east, south, north, jnp.where(z > 0, low, 0.0), jnp.where(z < length - 1, high, 0.0)
    )


def coarse_kernel(
    count_x, count_y, width, own, flat, res,
    coeffs, grid, halo_x, halo_y, ext,
    panel, gathered, faces, send_sem, recv_sem, halo_send, halo_recv
):
    index_x = lax.axis_index("gx")
    index_y = lax.axis_index("yz")
    count = count_x * count_y
    me = index_x * count_y + index_y
    fields, depth, breadth = own.shape[:3]
    parts = fields - 1
    rhs = res.shape[0]
    length = own.shape[4]
    barrier = pltpu.get_barrier_semaphore()
    zero = jnp.zeros((width, length), jnp.float32)

    def clear(x, carry):
        for f in range(fields):
            for y in range(breadth + 4):
                ext[f, x, y] = zero
        return carry

    lax.fori_loop(0, depth + 4, clear, 0)

    def greet(step, carry):
        other = lax.rem(me + step, count)
        pl.semaphore_signal(
            barrier, inc=1, device_id=(other // count_y, lax.rem(other, count_y)), device_id_type=MESH
        )
        return carry

    lax.fori_loop(1, count, greet, 0)

    def cut(r, carry):
        for f in range(parts):
            base = pl.multiple_of((r * parts + f) * depth * breadth, breadth)
            for side in range(2):
                faces[side, r, f] = flat[pl.ds(base + side * (breadth - 1), depth, stride=breadth), :]
        return carry

    lax.fori_loop(0, rhs, cut, 0)
    pl.semaphore_wait(barrier, count - 1)

    def can(dx, dy):
        ok = index_x >= 0
        if dx:
            ok = index_x > 0 if dx < 0 else index_x < count_x - 1
        if dy:
            ok_y = index_y > 0 if dy < 0 else index_y < count_y - 1
            ok = jnp.logical_and(ok, ok_y) if dx else ok_y
        return ok

    started = []

    def start(source, target, dx, dy):
        slot = len(started)
        copy = pltpu.make_async_remote_copy(
            src_ref=source,
            dst_ref=target,
            send_sem=halo_send.at[slot],
            recv_sem=halo_recv.at[slot],
            device_id=(index_x + dx, index_y + dy),
            device_id_type=MESH,
        )
        pl.when(can(dx, dy))(copy.start)
        started.append((can(dx, dy), can(-dx, -dy), copy))

    def layer(step):
        inner_x, inner_y = pl.ds(2, depth), pl.ds(2, breadth)
        start(own.at[:, step], ext.at[:, depth + 2 + step, inner_y], -1, 0)
        start(own.at[:, depth - 1 - step], ext.at[:, 1 - step, inner_y], 1, 0)
        start(own.at[:, :, step], ext.at[:, inner_x, breadth + 2 + step], 0, -1)
        start(own.at[:, :, breadth - 1 - step], ext.at[:, inner_x, 1 - step], 0, 1)

    def rows(low, count):
        part = pl.ds(low, count)
        start(res.at[part, :, 0], halo_x.at[1, part], -1, 0)
        start(res.at[part, :, depth - 1], halo_x.at[0, part], 1, 0)

    early = rhs * 3 // 8
    layer(0)
    first = len(started)
    rows(0, early)
    start(faces.at[0], halo_y.at[1], 0, -1)
    start(faces.at[1], halo_y.at[0], 0, 1)
    def fill(x, carry):
        for f in range(fields):
            for y in range(breadth):
                ext[f, x + 2, y + 2] = own[f, x, y]
        return carry

    lax.fori_loop(0, depth, fill, 0)

    cells = depth * breadth

    def loads(i, sums):
        f = i // depth
        x = i - f * depth
        base = pl.multiple_of(i * breadth, breadth)
        for y in range(breadth):
            v = own[f, x, y]
            sums = tuple(
                total + v * flat[pl.ds(base + r * parts * cells + y, 1), :]
                for r, total in enumerate(sums)
            )
        return sums

    sums = lax.fori_loop(0, parts * depth, loads, (zero,) * rhs)
    lane = lax.broadcasted_iota(jnp.int32, panel.shape, 1)

    def placed(total, at):
        return jnp.where(lane == at, jnp.sum(total, axis=1, keepdims=True), 0.0)

    size = count_y * width
    row = jnp.zeros(panel.shape, jnp.float32)
    for r in range(rhs):
        row = row + placed(sums[r], 3 * size + r)
    for _, receives, copy in started[:first]:
        pl.when(receives)(copy.wait_recv)

    def gram(sums, left, f, x, y):
        return tuple(
            total + left * ext[f, x, y, pl.ds(l, 1), :] for l, total in enumerate(sums)
        )

    def own_block(i, sums):
        inside_x = (
            jnp.where(i > 0, 1.0, 0.0).astype(jnp.float32),
            jnp.where(i < depth - 1, 1.0, 0.0).astype(jnp.float32),
        )
        x = i + 2
        for y in range(2, breadth + 2):
            _, diagonal, (west, east, south, north, low, high) = cell_weights(ext, x, y)
            west = west * inside_x[0]
            east = east * inside_x[1]
            for f in range(parts):
                v = ext[f, x, y]
                near = west * ext[f, x - 1, y] + east * ext[f, x + 1, y]
                if y > 2:
                    near = near + south * ext[f, x, y - 1]
                if y < breadth + 1:
                    near = near + north * ext[f, x, y + 1]
                near = near + low * pltpu.roll(v, 1, 1) + high * pltpu.roll(v, length - 1, 1)
                sums = gram(sums, diagonal * v - near, f, x, y)
        return sums

    def side_block(along, fixed_x, fixed_y, dx, dy):
        which = {(-1, 0): 0, (1, 0): 1, (0, -1): 2, (0, 1): 3}[(dx, dy)]

        def one(i, sums):
            x = i + 2 if fixed_x is None else fixed_x
            y = i + 2 if fixed_y is None else fixed_y
            weight = cell_weights(ext, x, y)[2][which]
            for f in range(parts):
                sums = gram(sums, -weight * ext[f, x, y], f, x + dx, y + dy)
            return sums

        return lax.fori_loop(0, along, one, (zero,) * width)

    blocks = (
        (lax.fori_loop(0, depth, own_block, (zero,) * width), index_y * width),
        (side_block(depth, None, 2, 0, -1), (index_y - 1) * width),
        (side_block(depth, None, breadth + 1, 0, 1), (index_y + 1) * width),
        (side_block(breadth, 2, None, -1, 0), size + index_y * width),
        (side_block(breadth, depth + 1, None, 1, 0), 2 * size + index_y * width),
    )
    for totals, at in blocks:
        for l in range(width):
            row = row + placed(totals[l], at + l)
    panel[...] = row
    gathered[me] = row

    def sending(other, slot):
        return pltpu.make_async_remote_copy(
            src_ref=panel,
            dst_ref=gathered.at[slot],
            send_sem=send_sem.at[other],
            recv_sem=recv_sem.at[slot],
            device_id=(other // count_y, lax.rem(other, count_y)),
            device_id_type=MESH,
        )

    def send(step, carry):
        sending(lax.rem(me + step, count), me).start()
        return carry

    lax.fori_loop(1, count, send, 0)
    rows(early, rhs - early)
    layer(1)
    ends_x = ((0, -1, depth + 2), (depth - 1, 1, 1))
    ends_y = ((0, -1, breadth + 2), (breadth - 1, 1, 1))
    for x, dx, to_x in ends_x:
        for y, dy, to_y in ends_y:
            start(own.at[:, x, y], ext.at[:, to_x, to_y], dx, dy)

    def collect(step, carry):
        other = lax.rem(me + step, count)
        sending(other, other).wait_recv()
        return carry

    lax.fori_loop(1, count, collect, 0)
    panels = [gathered[pl.ds(g * count_y, count_y)].reshape(size, length) for g in range(count_x)]
    for g, x in enumerate(cyclic_solve(panels, size)):
        coeffs[pl.ds(g * size, size), :] = x
    grid[...] = jnp.zeros(grid.shape, jnp.float32)
    slot = 0
    for step_x in (-1, 0, 1):
        for step_y in (-1, 0, 1):
            near_x = jnp.clip(index_x + step_x, 0, count_x - 1)
            near_y = jnp.clip(index_y + step_y, 0, count_y - 1)
            begin = pl.multiple_of((near_x * count_y + near_y) * width, width)
            grid[pl.ds(slot * width, width), pl.ds(0, rhs)] = coeffs[pl.ds(begin, width), :]
            slot += 1

    def drain(step, carry):
        sending(lax.rem(me + step, count), me).wait_send()
        return carry

    lax.fori_loop(1, count, drain, 0)
    for place, (sends, receives, copy) in enumerate(started):
        pl.when(sends)(copy.wait_send)
        if place >= first:
            pl.when(receives)(copy.wait_recv)


def coarse_solve(own, residuals, count_x, count_y):
    rhs, parts, depth, breadth, length = residuals.shape
    fields, width = own.shape[0], own.shape[3]
    count = count_x * count_y
    vmem = pl.BlockSpec(memory_space=pltpu.VMEM)
    hbm = pl.BlockSpec(memory_space=pl.ANY)
    panel = (width, 3 * count_y * width + rhs)
    return pl.pallas_call(
        functools.partial(coarse_kernel, count_x, count_y, width),
        out_shape=(
            jax.ShapeDtypeStruct((count * width, rhs), jnp.float32),
            jax.ShapeDtypeStruct((pl.cdiv(9 * width, 128) * 128, pl.cdiv(rhs, 128) * 128), jnp.float32),
            jax.ShapeDtypeStruct((2, rhs, parts, breadth, length), jnp.float32),
            jax.ShapeDtypeStruct((2, rhs, parts, depth, length), jnp.float32),
            jax.ShapeDtypeStruct((fields, depth + 4, breadth + 4, width, length), jnp.float32),
        ),
        in_specs=[vmem, vmem, hbm],
        out_specs=(vmem, vmem, hbm, hbm, vmem),
        scratch_shapes=[
            pltpu.VMEM(panel, jnp.float32),
            pltpu.VMEM((count,) + panel, jnp.float32),
            pltpu.VMEM((2, rhs, parts, depth, length), jnp.float32),
            pltpu.SemaphoreType.DMA((count,)),
            pltpu.SemaphoreType.DMA((count,)),
            pltpu.SemaphoreType.DMA((18,)),
            pltpu.SemaphoreType.DMA((18,)),
        ],
        compiler_params=pltpu.CompilerParams(collective_id=0, has_side_effects=True),
    )(
        own,
        residuals.reshape(-1, length),
        residuals,
    )


def schwarz_kernel(
    rhs, parts, depth, breadth, width, res_any, ext_any, cgrid, halo_x_any, halo_y_any, out_any, mine,
    res, ext, halo_x, halo_y, out, load_sem, ext_sem, out_sem,
    weights, coeff, corr, forced, first, second
):
    length = res.shape[1]
    wide = breadth + 4

    def load_field(f):
        return pltpu.make_async_copy(ext_any.at[f], ext.at[f], ext_sem.at[f])

    loads = [
        pltpu.make_async_copy(source, target, load_sem.at[i])
        for i, (source, target) in enumerate(((res_any, res), (halo_x_any, halo_x), (halo_y_any, halo_y)))
    ]
    for f in (parts, *range(parts)):
        load_field(f).start()
    for copy in loads:
        copy.start()
    own = depth * breadth

    mine[...] = cgrid[pl.ds(4 * width, width), pl.ds(0, rhs)]
    turned = cgrid[...].T
    for i in range(9 * width):
        coeff[i] = jnp.broadcast_to(turned[:rhs, i : i + 1], (rhs, length))
    zero = jnp.zeros((rhs, length), jnp.float32)
    for buffer in (forced, first, second):
        def clear_x(y, carry, buffer=buffer):
            buffer[y] = zero
            buffer[(depth + 3) * wide + y] = zero
            return carry

        def clear_y(x, carry, buffer=buffer):
            buffer[x * wide] = zero
            buffer[x * wide + wide - 1] = zero
            return carry

        lax.fori_loop(0, wide, clear_x, 0)
        lax.fori_loop(0, depth + 4, clear_y, 0)
        for x in (1, depth + 2):
            for y in (1, breadth + 2):
                buffer[x * wide + y] = zero

    load_field(parts).wait()

    def weigh(i, carry):
        for y in range(breadth + 2):
            m, diagonal, faces = cell_weights(ext, i + 1, y + 1)
            scale = jnp.where(m > 0, 0.8, 0.0) / diagonal
            at = i * (breadth + 2) + y
            weights[at, 0] = scale
            for q, w in enumerate(faces):
                weights[at, q + 1] = scale * w
        return carry

    lax.fori_loop(0, depth + 2, weigh, 0)

    def spread(w, q):
        return jnp.concatenate([weights[w, q]] * (rhs // width), axis=0)

    def component(part, carry):
        load_field(part).wait()

        def correct(cls, cells):
            values = [None] * len(cells)
            for k in range(width):
                c = coeff[cls * width + k]
                for i, (x, y) in enumerate(cells):
                    term = c * ext[part, x, y, pl.ds(k, 1), :]
                    values[i] = term if k == 0 else values[i] + term
            for (x, y), value in zip(cells, values):
                corr[x * wide + y] = value

        def along_y(cls, x0, nx):
            def one(i, carry):
                correct(cls, [(x0 + i, y + 2) for y in range(breadth)])
                return carry

            lax.fori_loop(0, nx, one, 0)

        def along_x(cls, y0):
            def one(i, carry):
                correct(cls, [(x + 2, y0 + i) for x in range(depth)])
                return carry

            lax.fori_loop(0, 2, one, 0)

        along_y(4, 2, depth)
        along_y(1, 0, 2)
        along_y(7, depth + 2, 2)
        along_x(3, 0)
        along_x(5, breadth + 2)
        for cls, x, y in (
            (0, 1, 1), (2, 1, breadth + 2), (6, depth + 2, 1), (8, depth + 2, breadth + 2)
        ):
            correct(cls, [(x, y)])

        def beside(buffer, x, y):
            cell = x * wide + y
            w = (x - 1) * (breadth + 2) + y - 1
            centre = buffer[cell]
            total = spread(w, 1) * buffer[cell - wide]
            total = total + spread(w, 2) * buffer[cell + wide]
            total = total + spread(w, 3) * buffer[cell - 1]
            total = total + spread(w, 4) * buffer[cell + 1]
            total = total + spread(w, 5) * pltpu.roll(centre, 1, 1)
            total = total + spread(w, 6) * pltpu.roll(centre, length - 1, 1)
            return centre, total

        def force(x, y, loaded, outer):
            cell = x * wide + y
            w = (x - 1) * (breadth + 2) + y - 1
            centre, total = beside(corr, x, y)
            scale = spread(w, 0)
            term = scale * loaded
            if outer:
                term = jnp.where(scale > 0, term, 0.0)
            forced[cell] = term - 0.8 * centre + total

        def force_row(i, carry):
            for y in range(breadth):
                start = part * own + i * breadth + y
                force(i + 2, y + 2, res[pl.ds(start, rhs, stride=parts * own), :], False)
            for side in range(2):
                start = side * rhs * parts * depth + part * depth + i
                loaded = halo_y[pl.ds(start, rhs, stride=parts * depth), :]
                force(i + 2, 1 + side * (breadth + 1), loaded, True)
            return carry

        @pl.when(part == 0)
        def _():
            for copy in loads:
                copy.wait()

        lax.fori_loop(0, depth, force_row, 0)

        def force_edge(i, carry):
            for side in range(2):
                start = side * rhs * parts * breadth + part * breadth + i
                loaded = halo_x[pl.ds(start, rhs, stride=parts * breadth), :]
                force(1 + side * (depth + 1), i + 2, loaded, True)
            return carry

        lax.fori_loop(0, breadth, force_edge, 0)

        source, target, spare = forced, first, second
        for sweep in range(1, SWEEPS):
            last = sweep == SWEEPS - 1

            def relaxed(x, y, source=source, opening=sweep == 1):
                centre, total = beside(source, x, y)
                if opening:
                    return 1.2 * centre + total
                return 0.2 * centre + (forced[x * wide + y] + total)

            def relax(x, y, target=target, relaxed=relaxed):
                target[x * wide + y] = relaxed(x, y)

            def finish(x, y, relaxed=relaxed):
                value = corr[x * wide + y] + relaxed(x, y)
                start = part * rhs * own + (x - 2) * breadth + y - 2
                out[pl.ds(start, rhs, stride=own), :] = value

            def row(i, carry, last=last, relax=relax, finish=finish):
                if last:
                    for y in range(breadth):
                        finish(i + 2, y + 2)
                else:
                    for y in range(breadth + 2):
                        relax(i + 2, y + 1)
                return carry

            lax.fori_loop(0, depth, row, 0)
            if not last:
                def edge(i, carry, relax=relax):
                    relax(1, i + 2)
                    relax(depth + 2, i + 2)
                    return carry

                lax.fori_loop(0, breadth, edge, 0)
            source, target, spare = target, spare, target

        def write(r, carry):
            pltpu.make_async_copy(
                out.at[pl.ds(pl.multiple_of((part * rhs + r) * own, own), own)],
                out_any.at[pl.ds(pl.multiple_of((r * parts + part) * own, own), own)],
                out_sem,
            ).start()
            return carry

        lax.fori_loop(0, rhs, write, 0)
        return carry

    lax.fori_loop(0, parts, component, 0)
    pltpu.make_async_copy(out, out_any, out_sem).wait()


def schwarz(residuals, ext, grid, halo_x, halo_y):
    rhs, parts, depth, breadth, length = residuals.shape
    width = ext.shape[3]
    vmem = pl.BlockSpec(memory_space=pltpu.VMEM)
    hbm = pl.BlockSpec(memory_space=pl.ANY)
    field = pltpu.VMEM(((depth + 4) * (breadth + 4), rhs, length), jnp.float32)
    result, coeffs = pl.pallas_call(
        functools.partial(schwarz_kernel, rhs, parts, depth, breadth, width),
        out_shape=(
            jax.ShapeDtypeStruct((rhs * parts * depth * breadth, length), jnp.float32),
            jax.ShapeDtypeStruct((width, rhs), jnp.float32),
        ),
        in_specs=[hbm, hbm, vmem, hbm, hbm],
        out_specs=(hbm, vmem),
        scratch_shapes=[
            pltpu.VMEM((residuals.size // length, length), jnp.float32),
            pltpu.VMEM(ext.shape, jnp.float32),
            pltpu.VMEM((halo_x.size // length, length), jnp.float32),
            pltpu.VMEM((halo_y.size // length, length), jnp.float32),
            pltpu.VMEM((residuals.size // length, length), jnp.float32),
            pltpu.SemaphoreType.DMA((3,)),
            pltpu.SemaphoreType.DMA((parts + 1,)),
            pltpu.SemaphoreType.DMA,
            pltpu.VMEM(((depth + 2) * (breadth + 2), 7, width, length), jnp.float32),
            pltpu.VMEM((9 * width, rhs, length), jnp.float32),
            field, field, field, field,
        ],
        compiler_params=pltpu.CompilerParams(vmem_limit_bytes=63 * 1024 * 1024),
    )(
        residuals.reshape(-1, length),
        ext,
        grid,
        halo_x.reshape(-1, length),
        halo_y.reshape(-1, length),
    )
    return coeffs, result.reshape(residuals.shape)


def on_device(residuals, vectors, phases, stiffness):
    count_x = lax.axis_size("gx")
    count_y = lax.axis_size("yz")
    width = vectors.shape[0]
    levels = stiffness.shape[0]
    choose = (phases[None] == jnp.arange(levels, dtype=jnp.int32)[:, None, None, None]).astype(
        jnp.float32
    )
    modulus = jnp.sum(stiffness[:, None, None, None] * choose, axis=0)
    spread = jnp.broadcast_to(modulus[None, :, :, None, :], (1,) + modulus.shape[:2] + (width, modulus.shape[2]))
    own = jnp.concatenate([vectors.transpose(1, 2, 3, 0, 4), spread], axis=0)
    _, grid, halo_x, halo_y, ext = coarse_solve(own, residuals, count_x, count_y)
    return schwarz(residuals, ext, grid, halo_x, halo_y)


def solution(mesh):
    return jax.shard_map(
        on_device,
        mesh=mesh,
        in_specs=(
            P(None, None, "gx", "yz", None),
            P(None, None, "gx", "yz", None),
            P("gx", "yz", None),
            P(),
        ),
        out_specs=(P(("gx", "yz"), None), P(None, None, "gx", "yz", None)),
        check_vma=False,
    )
```
